128 devices in a mesh: edge: 64 (over x, z, y), rep: 2 (over core).
Axes of the slice: x: 4, y: 4, z: 4, core: 2. Of those that a mesh axis runs over, the one named last changes fastest.
Arguments:
- edge_feats: bfloat16 [262144, 512], P(('rep', 'edge')), parts along dimension 0, may hold values from -6 to 6
- atom_feats: bfloat16 [32768, 512], P(('rep', 'edge')), parts along dimension 0, may hold values from -6 to 6
- w_edge: bfloat16 [6, 512, 512], replicated, may hold values from -0.25 to 0.25
- w_atom: bfloat16 [2, 512, 512], replicated, may hold values from -0.25 to 0.25
- send_order: int32 [128, 2048], P(('rep', 'edge')), parts along dimension 0, may hold values from 0 to 2047, as said below
- recv_pos: int32 [128, 2048], P(('rep', 'edge')), parts along dimension 0, may hold values from 0 to 2047, as said below
- edge_list: int32 [128, 2048], P(('rep', 'edge')), parts along dimension 0, may hold values from 0 to 31, never falling along the last dimension, each value on 1 to 192 neighbouring positions
- edge_atom: int32 [128, 2048], P(('rep', 'edge')), parts along dimension 0, may hold values from 0 to 127
- list_block: int32 [128, 32], P(('rep', 'edge')), parts along dimension 0, may hold values from 0 to 127, as said below
- block_home: int32 [256], P('rep'), parts along dimension 0, may hold values from 0 to 127, as said below
Outputs:
- edge_out: bfloat16 [262144, 512], P(('rep', 'edge')), parts along dimension 0
- atom_out: bfloat16 [32768, 512], P(('rep', 'edge')), parts along dimension 0
The draws below stay inside these ranges and needn't reach their ends.
There are 2 independent parts, one for each index of `rep`. The reference program is written for one: setup_inputs(seed, part) draws one part's arguments, and reference() takes and returns one part's arrays. A program takes and returns all parts, laid end to end along the dimension named above; an argument that names none is the same for every part. Nothing has to cross between parts.
Inputs may be any that keep to these rules, and one draw needn't show every extreme that they name: Each row of send_order is a permutation of the device's rows; each row of recv_pos is a permutation of the places. Every edge has exactly 32 reverse partners' messages passing between its device and each device, the pairing is symmetric, and no edge is its own partner. `recv_pos`: together with send_order the pairing of every edge with its reverse edge as described there. `list_block`: the 32 lists of one device aim at atom blocks stored on 32 different devices. `block_home`: A permutation of the block ids' storage positions.
All inputs are finite; a program needn't handle non-finite values.
Results may differ from the reference program's by a relative error of at most 0.0095.
Values may be sent and summed in bfloat16 or wider, within the bound.
A program may use at most 128 MiB of HBM per device.

```python
import math
import jax
import jax.numpy as jnp
import numpy as np
from jax import lax

H = 512
ABLK = 128
BLOCKS = 2
E_DEV = 2048
AB_DEV = 2
LISTS = 32
LIST_MOST = 192
CAP = 32
NB = 128
EDGES = 131072
N_EDGE = 64


def pairing(key):
    key = jax.random.fold_in(key, 11)
    keys = jax.random.split(key, N_EDGE)
    row_order = jax.vmap(lambda k: jax.random.permutation(k, E_DEV))(keys).astype(jnp.int32)
    slots = jnp.arange(E_DEV, dtype=jnp.int32)
    group = slots // CAP
    within = slots % CAP
    devices = jnp.arange(N_EDGE, dtype=jnp.int32)[:, None]
    places = jnp.where(group[None, :] == devices, group[None, :] * CAP + CAP - 1 - within[None, :], slots[None, :])
    received = jnp.zeros((N_EDGE, E_DEV), jnp.int32).at[devices, row_order].set(places.astype(jnp.int32))
    return (row_order, received)


def placing(key):
    key = jax.random.fold_in(key, 23)
    first_key, second_key, third_key = jax.random.split(key, 3)
    home = jax.random.permutation(first_key, NB).astype(jnp.int32)
    inverse = jnp.zeros((NB,), jnp.int32).at[home].set(jnp.arange(NB, dtype=jnp.int32))
    keys = jax.random.split(second_key, N_EDGE)
    owners = jax.vmap(lambda k: jax.random.permutation(k, N_EDGE)[:LISTS])(keys).astype(jnp.int32)
    slots = jax.random.randint(third_key, (N_EDGE, LISTS), 0, AB_DEV).astype(jnp.int32)
    blocks = inverse[owners * AB_DEV + slots]
    return (blocks, home)


def draw_send_order(key, part):
    return pairing(key)[0]


def draw_recv_pos(key, part):
    return pairing(key)[1]


def draw_list_block(key, part):
    return placing(key)[0]


def draw_block_home(key, part):
    return placing(key)[1]


def plant(drawn, stream_key, least, largest):
    longest = drawn.shape.index(max(drawn.shape))
    spots = []
    for shift in (0, 1):
        where = [jax.random.randint(jax.random.fold_in(stream_key, axis), (), 0, length) for axis, length in enumerate(drawn.shape)]
        where[longest] = (where[longest] + shift) % drawn.shape[longest]
        spots.append(tuple(where))
    return drawn.at[spots[0]].set(least).at[spots[1]].set(largest)


def shard_levels(own_key, shape, shards, low, top_value):
    def one(dim, shards_of):
        heights = jax.random.uniform(jax.random.fold_in(jax.random.fold_in(own_key, 6), dim), (shards_of,), jnp.float32, low / len(shards), top_value / len(shards))
        return jnp.repeat(jnp.exp(heights), shape[dim] // shards_of).reshape((-1,) + (1,) * (len(shape) - dim - 1))

    factor_of = one(*shards[0])
    for cut in shards[1:]:
        factor_of = factor_of * one(*cut)
    return factor_of


def length_profile(count, total, bound, lean):
    loads = [(1 << 20) // math.isqrt(rank ** lean) + 1 for rank in range(2, count + 1)]
    rest, holding = total - bound - (count - 1), [1] * (count - 1)
    while rest > 0:
        candidates = [i for i in range(count - 1) if holding[i] < bound]
        mass, remaining = sum([loads[i] for i in candidates]), rest
        for i in candidates:
            addition = min(bound - holding[i], max(1, remaining * loads[i] // mass), rest)
            holding[i] = holding[i] + addition
            rest = rest - addition
    return np.array([bound] + holding)


def ragged(own_key, count, total, bound, skew):
    if count == 2:
        one = jax.random.randint(own_key, (), max(1, total - bound), min(bound, total - 1) + 1)
        return jnp.stack([one, total - one])
    tallies = jnp.asarray(length_profile(count, total, bound, skew), jnp.int32)
    couples = (count - 1) // 2
    source_of, sink = tallies[1:1 + 2 * couples:2], tallies[2:2 + 2 * couples:2]
    slack = jnp.minimum(source_of - 1, bound - sink)
    passed = jax.random.randint(jax.random.fold_in(own_key, 1), (couples,), 0, 1 << 20) % (slack + 1)
    tallies = tallies.at[1:1 + 2 * couples:2].set(source_of - passed).at[2:2 + 2 * couples:2].set(sink + passed)
    return tallies[jax.random.permutation(jax.random.fold_in(own_key, 2), count)]


def gaussian(stream_key, shape, spread, most, cuts=(), kind=jnp.bfloat16):
    drawn = jax.random.normal(stream_key, shape, jnp.float32) * spread
    if len(cuts) > 0:
        drawn = shard_levels(stream_key, shape, cuts, -0.22, 0.18) * drawn
    return jnp.clip(drawn, min=-most, max=most).astype(kind)


def setup_inputs(seed: int = 0, part: int = 0) -> dict:
    arg_keys = jax.random.split(jax.random.key(seed), 11)
    part_splits = jax.random.split(jax.random.fold_in(arg_keys[10], part), 11)
    edge_feats = gaussian(part_splits[0], (EDGES, H), 1.0, 6.0, ((0, 64),))
    atom_feats = gaussian(part_splits[1], (NB * ABLK, H), 1.0, 6.0, ((0, 64),))
    w_edge = gaussian(arg_keys[2], (3 * BLOCKS, H, H), H ** -0.5, 0.25)
    w_atom = gaussian(arg_keys[3], (BLOCKS, H, H), H ** -0.5, 0.25)
    send_order = draw_send_order(jax.random.fold_in(jax.random.fold_in(arg_keys[10], part), 71), part)
    recv_pos = draw_recv_pos(jax.random.fold_in(jax.random.fold_in(arg_keys[10], part), 71), part)
    edge_list = jax.vmap(lambda own: jnp.searchsorted(jnp.cumsum(ragged(own, LISTS, E_DEV, LIST_MOST, 2)), jnp.arange(E_DEV), side="right"))(jax.random.split(part_splits[6], N_EDGE)).reshape((N_EDGE, E_DEV)).astype(jnp.int32)
    edge_atom = plant(jax.random.randint(part_splits[7], (N_EDGE, E_DEV), 0, ABLK), jax.random.fold_in(part_splits[7], 1), 0, ABLK - 1).astype(jnp.int32)
    list_block = draw_list_block(jax.random.fold_in(jax.random.fold_in(arg_keys[10], part), 71), part)
    block_home = draw_block_home(jax.random.fold_in(jax.random.fold_in(arg_keys[10], part), 71), part)
    return {"edge_feats": edge_feats, "atom_feats": atom_feats, "w_edge": w_edge, "w_atom": w_atom, "send_order": send_order, "recv_pos": recv_pos, "edge_list": edge_list, "edge_atom": edge_atom, "list_block": list_block, "block_home": block_home}


def dense_silu(values, weight):
    return jax.nn.silu(jnp.dot(values, weight, preferred_element_type=jnp.float32)).astype(jnp.bfloat16)


def reference(edge_feats, atom_feats, w_edge, w_atom, send_order, recv_pos, edge_list, edge_atom, list_block, block_home):
    devices = jnp.arange(N_EDGE, dtype=jnp.int32)[:, None]
    source = recv_pos // CAP
    within = recv_pos % CAP
    source_row = send_order[source, devices * CAP + within]
    partner = (source * E_DEV + source_row).reshape(-1).astype(jnp.int32)
    list_pos = block_home[list_block]
    edge_pos = jnp.take_along_axis(list_pos, edge_list, axis=1)
    target = (edge_pos * ABLK + edge_atom).reshape(-1).astype(jnp.int32)
    seg_keys = (edge_list * ABLK + edge_atom).astype(jnp.int32)
    message = edge_feats
    atoms = atom_feats
    for layer_block in range(BLOCKS):
        first = dense_silu(message, w_edge[3 * layer_block])
        second = dense_silu(first, w_edge[3 * layer_block + 1])
        paired = (second.astype(jnp.float32) + second[partner].astype(jnp.float32)).astype(jnp.bfloat16)
        third = dense_silu(paired, w_edge[3 * layer_block + 2])

        def add_device(total, items):
            rows, keys, places = items
            part = jax.ops.segment_sum(rows.astype(jnp.float32), keys, num_segments=LISTS * ABLK)
            part = part.astype(jnp.bfloat16).astype(jnp.float32).reshape(LISTS, ABLK, H)
            return total.at[places].add(part), None

        start = jnp.zeros((NB, ABLK, H), jnp.float32)
        gathered, _ = lax.scan(add_device, start, (third.reshape(N_EDGE, E_DEV, H), seg_keys, list_pos))
        gathered = gathered.reshape(NB * ABLK, H).astype(jnp.bfloat16)
        update = jax.nn.silu(jnp.dot(gathered, w_atom[layer_block], preferred_element_type=jnp.float32))
        atoms = (atoms.astype(jnp.float32) + update).astype(jnp.bfloat16)
        message = (message.astype(jnp.float32) + third.astype(jnp.float32) + atoms[target].astype(jnp.float32)).astype(jnp.bfloat16)
    return message, atoms
```

```python
import functools

import jax
import jax.numpy as jnp
from jax import lax
from jax.experimental import pallas as pl
from jax.experimental.pallas import tpu as pltpu
from jax.sharding import PartitionSpec as P

ABLK = 128
BLOCKS = 2
AB_DEV = 2
SIDE = 4
PEERS = SIDE * SIDE * SIDE
STRIDES = (16, 4, 1)
GROUP_AXES = ((0, 1, 2), (1, 2, 0), (2, 0, 1))
GROUP_ROWS = ((0, 176), (176, 176), (352, 160))
MESH = pl.DeviceIdType.MESH
F32 = jnp.float32
BF16 = jnp.bfloat16


def silu(v):
    return v / (1.0 + jnp.exp(-v))


def coords(me):
    return [(me // s) % SIDE for s in STRIDES]


def moved(me, place, axis, step):
    new = (place[axis] + step) % SIDE
    return me + (new - place[axis]) * STRIDES[axis], new


def peer_at(me, i, sign):
    i0, i1, i2 = i % 4, (i // 4) % 4, i // 16
    dx, dz, dy = i0, i1 + i0, i2 + i1 + i0
    px = (me // 16 + sign * dx + 16) % 4
    pz = ((me // 4) % 4 + sign * dz + 16) % 4
    py = (me % 4 + sign * dy + 16) % 4
    return px * 16 + pz * 4 + py


def exchange_kernel(
    layer_block,
    msg,
    w_hbm,
    order,
    places,
    ids,
    paired,
    ids_out,
    weights,
    second,
    outgoing,
    arrived,
    total,
    w_sem,
    send_sem,
    recv_sem,
    id_send,
    id_recv,
):
    me = lax.axis_index("edge")
    rep = lax.axis_index("rep")
    place = coords(me)
    barrier = pltpu.get_barrier_semaphore()

    def greet(i, carry):
        pl.semaphore_signal(barrier, inc=1, device_id=(peer_at(me, i, 1), rep), device_id_type=MESH)
        return carry

    lax.fori_loop(1, PEERS, greet, 0)
    load = pltpu.make_async_copy(w_hbm.at[pl.ds(3 * layer_block, 2)], weights, w_sem)
    load.start()
    load.wait()

    def dense(c, carry):
        rows = pl.ds(pl.multiple_of(c * 256, 256), 256)
        first = silu(jnp.dot(msg[rows, :], weights[0], preferred_element_type=F32)).astype(BF16)
        value = silu(jnp.dot(first, weights[1], preferred_element_type=F32)).astype(BF16)
        second[rows, :] = value
        return carry

    lax.fori_loop(0, 8, dense, 0)
    pl.semaphore_wait(barrier, PEERS - 1)

    id_copies = []
    for axis in range(3):
        ids_out[pl.ds(axis * SIDE + place[axis], 1)] = ids[...][None]
        for step in range(1, SIDE):
            peer, _ = moved(me, place, axis, step)
            copy = pltpu.make_async_remote_copy(
                src_ref=ids,
                dst_ref=ids_out.at[axis * SIDE + place[axis]],
                send_sem=id_send.at[axis * 3 + step - 1],
                recv_sem=id_recv.at[axis * 3 + step - 1],
                device_id=(peer, rep),
                device_id_type=MESH,
            )
            copy.start()
            id_copies.append(copy)

    def message(i):
        return pltpu.make_async_remote_copy(
            src_ref=outgoing.at[pl.ds(pl.multiple_of(i * 32, 32), 32)],
            dst_ref=arrived.at[pl.ds(pl.multiple_of(i * 32, 32), 32)],
            send_sem=send_sem.at[i],
            recv_sem=recv_sem.at[i],
            device_id=(peer_at(me, i, 1), rep),
            device_id_type=MESH,
        )

    def send_chunk(c, carry):
        wanted = jnp.concatenate(
            [
                order[pl.ds(pl.multiple_of(peer_at(me, c * 8 + j, 1) * 32, 32), 32), :]
                for j in range(8)
            ],
            axis=0,
        )
        pick = (wanted == lax.broadcasted_iota(jnp.int32, (256, 2048), 1)).astype(F32).astype(BF16)
        rows = jnp.dot(pick, second[...], preferred_element_type=F32).astype(BF16)
        outgoing[pl.ds(pl.multiple_of(c * 256, 256), 256), :] = rows

        def start(j, inner):
            message(c * 8 + j).start()
            return inner

        @pl.when(c == 0)
        def _():
            arrived[0:32, :] = rows[0:32, :]
            lax.fori_loop(1, 8, start, 0)

        @pl.when(c > 0)
        def _():
            lax.fori_loop(0, 8, start, 0)

        return carry

    lax.fori_loop(0, 8, send_chunk, 0)

    def take_chunk(c, carry):
        def arrive(j, inner):
            @pl.when(c * 8 + j > 0)
            def _():
                message(c * 8 + j).wait_recv()

            return inner

        lax.fori_loop(0, 8, arrive, 0)
        lane = lax.broadcasted_iota(jnp.int32, (1, 256), 1)
        source = peer_at(me, c * 8 + lane // 32, -1) * 32 + lane % 32
        block = arrived[pl.ds(pl.multiple_of(c * 256, 256), 256), :]

        def add(r, inner):
            rows = pl.ds(pl.multiple_of(r * 256, 256), 256)
            pick = (places[rows, :] == source).astype(F32).astype(BF16)
            value = jnp.dot(pick, block, preferred_element_type=F32)

            @pl.when(c == 0)
            def _():
                total[rows, :] = second[rows, :].astype(F32) + value

            @pl.when((c > 0) & (c < 7))
            def _():
                total[rows, :] += value

            @pl.when(c == 7)
            def _():
                paired[rows, :] = (total[rows, :] + value).astype(BF16)

            return inner

        lax.fori_loop(0, 8, add, 0)
        return carry

    lax.fori_loop(0, 8, take_chunk, 0)

    def finish(i, carry):
        message(i).wait_send()
        return carry

    lax.fori_loop(1, PEERS, finish, 0)
    for copy in id_copies:
        copy.wait()


def exchange(layer_block, message, w_edge, order, places, ids):
    rows, feat = message.shape
    vmem = pl.BlockSpec(memory_space=pltpu.VMEM)
    return pl.pallas_call(
        functools.partial(exchange_kernel, layer_block),
        out_shape=(
            jax.ShapeDtypeStruct((rows, feat), BF16),
            jax.ShapeDtypeStruct((3 * SIDE, 8, 128), jnp.int32),
        ),
        in_specs=[vmem, pl.BlockSpec(memory_space=pl.ANY), vmem, vmem, vmem],
        out_specs=(vmem, vmem),
        scratch_shapes=[
            pltpu.VMEM((2, feat, feat), BF16),
            pltpu.VMEM((rows, feat), BF16),
            pltpu.VMEM((rows, feat), BF16),
            pltpu.VMEM((rows, feat), BF16),
            pltpu.VMEM((rows, feat), F32),
            pltpu.SemaphoreType.DMA,
            pltpu.SemaphoreType.DMA((PEERS,)),
            pltpu.SemaphoreType.DMA((PEERS,)),
            pltpu.SemaphoreType.DMA((9,)),
            pltpu.SemaphoreType.DMA((9,)),
        ],
        name=f"exchange{layer_block}",
        compiler_params=pltpu.CompilerParams(collective_id=layer_block, has_side_effects=True),
    )(message, w_edge, order, places, ids)


def sums_kernel(layer_block, list_of, start, stop, pair, w_edge, keys, third, out, acc):
    step = pl.program_id(0)

    @pl.when(step == 0)
    def _():
        def dense(c, carry):
            rows = pl.ds(pl.multiple_of(c * 256, 256), 256)
            value = silu(jnp.dot(pair[rows, :], w_edge[0], preferred_element_type=F32))
            third[rows, :] = value.astype(BF16)
            return carry

        lax.fori_loop(0, 8, dense, 0)

    def one(j, carry):
        which = list_of[step * 8 + j]

        @pl.when(which < 0)
        def _():
            out[j] = jnp.zeros(out.shape[1:], BF16)

        @pl.when(which >= 0)
        def _():
            begin = start[which] // 128
            end = (stop[which] - 1) // 128
            want = which * ABLK + lax.broadcasted_iota(jnp.int32, (ABLK, 128), 0)

            def tile(t):
                pick = (keys[pl.ds(t, 1), :] == want).astype(F32).astype(BF16)
                rows = third[pl.ds(pl.multiple_of(t * 128, 128), 128), :]
                return jnp.dot(pick, rows, preferred_element_type=F32)

            acc[...] = tile(begin)

            def more(t, inner):
                acc[...] += tile(t)
                return inner

            lax.fori_loop(begin + 1, end + 1, more, 0)
            for k in range(4):
                out[j, k * 128 : (k + 1) * 128, :] = acc[:, k * 128 : (k + 1) * 128].astype(BF16)

        return carry

    lax.fori_loop(0, 8, one, 0)


def list_sums(layer_block, pair, w_edge, keys, list_of, start, stop):
    rows, feat = pair.shape
    return pl.pallas_call(
        functools.partial(sums_kernel, layer_block),
        out_shape=(
            jax.ShapeDtypeStruct((rows, feat), BF16),
            jax.ShapeDtypeStruct((PEERS, 512, 128), BF16),
        ),
        grid_spec=pltpu.PrefetchScalarGridSpec(
            num_scalar_prefetch=3,
            grid=(8,),
            in_specs=[
                pl.BlockSpec((rows, feat), lambda i, *_: (0, 0)),
                pl.BlockSpec((1, feat, feat), lambda i, *_: (3 * layer_block + 2, 0, 0)),
                pl.BlockSpec((16, 128), lambda i, *_: (0, 0)),
            ],
            out_specs=[
                pl.BlockSpec((rows, feat), lambda i, *_: (0, 0)),
                pl.BlockSpec((8, 512, 128), lambda i, *_: (i, 0, 0)),
            ],
            scratch_shapes=[pltpu.VMEM((ABLK, feat), F32)],
        ),
        name=f"sums{layer_block}",
        compiler_params=pltpu.CompilerParams(dimension_semantics=("arbitrary",)),
    )(list_of, start, stop, pair, w_edge, keys)


def atoms_kernel(layer_block, bits, sums, w_hbm, atoms, home, atoms_out, *scratch):
    names = ["r1", "t1", "r2", "t2", "r3", "fan", "sel"]
    bufs = {name: scratch[3 * n : 3 * n + 3] for n, name in enumerate(names)}
    flat, weight, w_sem, own_sem, s1, q1, s2, q2, s3, q3, s4, q4, s5, q5, s6, q6, out_sem = scratch[21:]
    me = lax.axis_index("edge")
    rep = lax.axis_index("rep")
    place = coords(me)
    barrier = pltpu.get_barrier_semaphore()
    for axis in range(3):
        for step in range(1, SIDE):
            peer, _ = moved(me, place, axis, step)
            pl.semaphore_signal(barrier, inc=1, device_id=(peer, rep), device_id_type=MESH)
    load = pltpu.make_async_copy(w_hbm.at[layer_block], weight, w_sem)
    load.start()

    def spot(g, va, vb, vc):
        index = [None] * 3
        for axis, value in zip(GROUP_AXES[g], (va, vb, vc)):
            index[axis] = value
        return tuple(index)

    def number(g, va, vb, vc):
        x, z, y = spot(g, va, vb, vc)
        return x * 16 + z * 4 + y

    def rows_of(g):
        return pl.ds(GROUP_ROWS[g][0], GROUP_ROWS[g][1])

    every = pl.ds(0, SIDE)
    send = pltpu.make_async_remote_copy
    here = [[place[axis] for axis in GROUP_AXES[g]] for g in range(3)]
    started = []

    own_copies = {}
    for j in range(SIDE):
        for g in range(3):
            ha, hb, hc = here[g]
            vb = (hb + 1 + j) % SIDE
            copy = pltpu.make_async_copy(
                sums.at[spot(g, ha, vb, every) + (rows_of(g),)], bufs["r1"][g].at[0, j], own_sem.at[g, j]
            )
            copy.start()
            own_copies[g, j] = copy
    pl.semaphore_wait(barrier, 9)

    in1 = {}
    for j in range(SIDE):
        for k in (2, 1, 3):
            for g in range(3):
                ha, hb, hc = here[g]
                peer, va = moved(me, place, GROUP_AXES[g][0], k)
                vb = (hb + 1 + j) % SIDE
                copy = send(
                    src_ref=sums.at[spot(g, va, vb, every) + (rows_of(g),)],
                    dst_ref=bufs["r1"][g].at[k, j],
                    send_sem=s1.at[g, k, j],
                    recv_sem=q1.at[g, k, j],
                    device_id=(peer, rep),
                    device_id_type=MESH,
                )
                copy.start()
                in1[g, k, j] = copy
                started.append(copy)

    in2 = {}
    for j in range(SIDE):
        for g in range(3):
            ha, hb, hc = here[g]
            n = GROUP_ROWS[g][1]
            axis_a = GROUP_AXES[g][0]
            vb = (hb + 1 + j) % SIDE
            own_copies[g, j].wait()
            for k in range(1, SIDE):
                in1[g, k, j].wait_recv()
            r1, t1 = bufs["r1"][g], bufs["t1"][g]

            def one(m, carry, g=g, j=j, ha=ha, hb=hb, hc=hc, vb=vb, axis_a=axis_a, r1=r1, t1=t1, n=n):
                dest = number(g, ha, vb, m)
                low = jnp.zeros((n, 128), F32)
                high = jnp.zeros((n, 128), F32)
                for k in range(SIDE):
                    source = (ha - k + SIDE) % SIDE
                    bit = bits[axis_a * SIDE + source, dest].astype(F32)
                    value = r1[k, j, m].astype(F32)
                    upper = value * bit
                    high = high + upper
                    low = low + (value - upper)
                t1[j, m, 0] = low.astype(BF16)
                t1[j, m, 1] = high.astype(BF16)
                return carry

            lax.fori_loop(0, SIDE, one, 0)
            if j < SIDE - 1:
                peer, _ = moved(me, place, GROUP_AXES[g][1], 1 + j)
                for i in range(SIDE):
                    vc = (hc + 1 + i) % SIDE
                    copy = send(
                        src_ref=t1.at[j, vc],
                        dst_ref=bufs["r2"][g].at[j, vc],
                        send_sem=s2.at[g, j, i],
                        recv_sem=q2.at[g, j, i],
                        device_id=(peer, rep),
                        device_id_type=MESH,
                    )
                    copy.start()
                    in2[g, j, i] = copy
                    started.append(copy)

    in3 = {}
    for i in range(SIDE):
        for g in range(3):
            ha, hb, hc = here[g]
            vc = (hc + 1 + i) % SIDE
            for j in range(SIDE - 1):
                in2[g, j, i].wait_recv()
            t1, r2, t2 = bufs["t1"][g], bufs["r2"][g], bufs["t2"][g]
            for slot in range(AB_DEV):
                value = t1[SIDE - 1, vc, slot].astype(F32)
                for j in range(SIDE - 1):
                    value = value + r2[j, vc, slot].astype(F32)
                t2[i, slot] = value.astype(BF16)
            if i < SIDE - 1:
                peer, _ = moved(me, place, GROUP_AXES[g][2], 1 + i)
                copy = send(
                    src_ref=t2.at[i],
                    dst_ref=bufs["r3"][g].at[i],
                    send_sem=s3.at[g, i],
                    recv_sem=q3.at[g, i],
                    device_id=(peer, rep),
                    device_id_type=MESH,
                )
                copy.start()
                in3[g, i] = copy
                started.append(copy)

    for g in range(3):
        for i in range(SIDE - 1):
            in3[g, i].wait_recv()
        t2, r3 = bufs["t2"][g], bufs["r3"][g]
        for slot in range(AB_DEV):
            value = t2[SIDE - 1, slot].astype(F32)
            for i in range(SIDE - 1):
                value = value + r3[i, slot].astype(F32)
            flat[slot, rows_of(g), :] = value.astype(BF16)

    load.wait()
    for slot in range(AB_DEV):
        gathered = jnp.concatenate([flat[slot, k * 128 : (k + 1) * 128, :] for k in range(4)], axis=1)
        update = silu(jnp.dot(gathered, weight[...], preferred_element_type=F32))
        rows = slice(slot * ABLK, (slot + 1) * ABLK)
        fresh = (atoms[rows, :].astype(F32) + update).astype(BF16)
        atoms_out[rows, :] = fresh
        for k in range(4):
            flat[slot, k * 128 : (k + 1) * 128, :] = fresh[:, k * 128 : (k + 1) * 128]
    in4 = {}
    for g in range(3):
        fan = bufs["fan"][g]
        fan[0, 0] = flat[:, rows_of(g), :]
        for k in (2, 1, 3):
            peer, _ = moved(me, place, GROUP_AXES[g][2], k)
            copy = send(
                src_ref=fan.at[0, 0],
                dst_ref=fan.at[0, k],
                send_sem=s4.at[g, k],
                recv_sem=q4.at[g, k],
                device_id=(peer, rep),
                device_id_type=MESH,
            )
            copy.start()
            in4[g, k] = copy
            started.append(copy)

    in5 = {}
    for i in (0, 1, 3, 2):
        for g in range(3):
            fan = bufs["fan"][g]
            if i:
                in4[g, i].wait_recv()
            for k in (2, 1, 3):
                peer, _ = moved(me, place, GROUP_AXES[g][1], k)
                copy = send(
                    src_ref=fan.at[0, i],
                    dst_ref=fan.at[k, i],
                    send_sem=s5.at[g, k, i],
                    recv_sem=q5.at[g, k, i],
                    device_id=(peer, rep),
                    device_id_type=MESH,
                )
                copy.start()
                in5[g, k, i] = copy
                started.append(copy)

    out_copies = []
    in6 = []
    for j in (0, 1, 3, 2):
        for g in range(3):
            ha, hb, hc = here[g]
            fan, sel = bufs["fan"][g], bufs["sel"][g]
            axis_a = GROUP_AXES[g][0]
            if j:
                for i in range(SIDE):
                    in5[g, j, i].wait_recv()
            vb = (hb - j + SIDE) % SIDE

            def choose(m, carry, g=g, j=j, ha=ha, hc=hc, vb=vb, axis_a=axis_a, fan=fan, sel=sel):
                vc = (hc - m + SIDE) % SIDE
                dest = number(g, ha, vb, vc)
                for k in range(SIDE):
                    bit = bits[axis_a * SIDE + (ha + k) % SIDE, dest]
                    sel[k, j, vc] = jnp.where(bit > 0, fan[j, m, 1], fan[j, m, 0])
                return carry

            lax.fori_loop(0, SIDE, choose, 0)
            target = home.at[spot(g, ha, vb, every) + (rows_of(g),)]
            for k in (2, 1, 3):
                peer, _ = moved(me, place, axis_a, k)
                copy = send(
                    src_ref=sel.at[k, j],
                    dst_ref=target,
                    send_sem=s6.at[g, k, j],
                    recv_sem=q6.at[g, k, j],
                    device_id=(peer, rep),
                    device_id_type=MESH,
                )
                copy.start()
                in6.append(copy)
                started.append(copy)
            copy = pltpu.make_async_copy(sel.at[0, j], target, out_sem.at[g, j])
            copy.start()
            out_copies.append(copy)

    for copy in out_copies:
        copy.wait()
    for copy in in6:
        copy.wait_recv()
    for copy in started:
        copy.wait_send()


def atom_round(layer_block, sums, w_atom, atoms, bits):
    feat = atoms.shape[1]
    vmem = pl.BlockSpec(memory_space=pltpu.VMEM)
    anywhere = pl.BlockSpec(memory_space=pl.ANY)

    def per_group(*lead):
        return [pltpu.VMEM(lead + (n, 128), BF16) for _, n in GROUP_ROWS]

    dma = pltpu.SemaphoreType.DMA
    scratch = (
        per_group(4, 4, 4)
        + per_group(4, 4, 2)
        + per_group(3, 4, 2)
        + per_group(4, 2)
        + per_group(3, 2)
        + per_group(4, 4, 2)
        + per_group(4, 4, 4)
        + [
            pltpu.VMEM((2, 512, 128), BF16),
            pltpu.VMEM((feat, feat), BF16),
            dma,
            dma((3, 4)),
            dma((3, 4, 4)),
            dma((3, 4, 4)),
            dma((3, 3, 4)),
            dma((3, 3, 4)),
            dma((3, 3)),
            dma((3, 3)),
            dma((3, 4)),
            dma((3, 4)),
            dma((3, 4, 4)),
            dma((3, 4, 4)),
            dma((3, 4, 4)),
            dma((3, 4, 4)),
            dma((3, 4)),
        ]
    )
    home, fresh = pl.pallas_call(
        functools.partial(atoms_kernel, layer_block),
        out_shape=(
            jax.ShapeDtypeStruct((SIDE, SIDE, SIDE, 512, 128), BF16),
            jax.ShapeDtypeStruct(atoms.shape, BF16),
        ),
        in_specs=[pl.BlockSpec(memory_space=pltpu.SMEM), anywhere, anywhere, vmem],
        out_specs=(anywhere, vmem),
        scratch_shapes=scratch,
        name=f"atoms{layer_block}",
        compiler_params=pltpu.CompilerParams(
            collective_id=BLOCKS + layer_block, has_side_effects=True, vmem_limit_bytes=56 << 20
        ),
    )(bits, sums.reshape(SIDE, SIDE, SIDE, 512, 128), w_atom, atoms)
    return home.reshape(PEERS, 512, 128), fresh


def fetch_kernel(owner, first, last, msg, third, keys, home, out, blocks, acc, sems):
    count = owner.shape[0]

    def copy(l):
        return pltpu.make_async_copy(home.at[owner[l]], blocks.at[l], sems.at[l])

    def begin(l, carry):
        copy(l).start()
        return carry

    lax.fori_loop(0, count, begin, 0)

    def finish(l, carry):
        copy(l).wait()
        return carry

    lax.fori_loop(0, count, finish, 0)

    def tile(t, carry):
        rows = pl.ds(pl.multiple_of(t * 128, 128), 128)
        acc[...] = msg[rows, :].astype(F32) + third[rows, :].astype(F32)

        def add(l, inner):
            want = l * ABLK + lax.broadcasted_iota(jnp.int32, (128, ABLK), 1)
            pick = (keys[rows, :] == want).astype(F32).astype(BF16)
            block = jnp.concatenate([blocks[l, k * 128 : (k + 1) * 128, :] for k in range(4)], axis=1)
            acc[...] += jnp.dot(pick, block, preferred_element_type=F32)
            return inner

        lax.fori_loop(first[t], last[t] + 1, add, 0)
        out[rows, :] = acc[...].astype(BF16)
        return carry

    lax.fori_loop(0, 16, tile, 0)


def fetch(message, third, keys, home, owner, first, last):
    rows, feat = message.shape
    lists = owner.shape[0]
    vmem = pl.BlockSpec(memory_space=pltpu.VMEM)
    smem = pl.BlockSpec(memory_space=pltpu.SMEM)
    return pl.pallas_call(
        fetch_kernel,
        out_shape=jax.ShapeDtypeStruct((rows, feat), BF16),
        in_specs=[smem, smem, smem, vmem, vmem, vmem, pl.BlockSpec(memory_space=pl.ANY)],
        out_specs=vmem,
        scratch_shapes=[
            pltpu.VMEM((lists, 512, 128), BF16),
            pltpu.VMEM((128, feat), F32),
            pltpu.SemaphoreType.DMA((lists,)),
        ],
        name="fetch",
    )(owner, first, last, message, third, keys, home)


def on_device(
    edge_feats,
    atom_feats,
    w_edge,
    w_atom,
    send_order,
    recv_pos,
    edge_list,
    edge_atom,
    list_block,
    block_home,
):
    lists = list_block.shape[1]
    list_table = jnp.arange(lists, dtype=jnp.int32)
    peer_table = jnp.arange(PEERS, dtype=jnp.int32)
    block_table = jnp.arange(block_home.shape[0], dtype=jnp.int32)
    list_place = jnp.sum(
        jnp.where(list_block[0][:, None] == block_table[None, :], block_home[None, :], 0), axis=1
    )
    owner = list_place // AB_DEV
    placing = owner[None, :] == peer_table[:, None]
    list_of = jnp.max(jnp.where(placing, list_table[None, :], -1), axis=1)
    slot_of = jnp.sum(jnp.where(placing, (list_place % AB_DEV)[None, :], 0), axis=1)
    edge_lists = edge_list[0]
    start = jnp.sum((edge_lists[None, :] < list_table[:, None]).astype(jnp.int32), axis=1)
    stop = jnp.sum((edge_lists[None, :] <= list_table[:, None]).astype(jnp.int32), axis=1)
    tiled_lists = edge_lists.reshape(16, 128)
    first, last = tiled_lists[:, 0], tiled_lists[:, 127]
    keys = edge_lists * ABLK + edge_atom[0]
    keys_row = keys.reshape(16, 128)
    keys_col = keys.reshape(-1, 1)
    order = send_order.reshape(-1, 1)
    places = recv_pos.reshape(-1, 1)
    ids = jnp.broadcast_to(jnp.pad(slot_of, (0, 128 - PEERS))[None, :], (8, 128))
    message, atoms = edge_feats, atom_feats
    for layer_block in range(BLOCKS):
        pair, all_ids = exchange(layer_block, message, w_edge, order, places, ids)
        if layer_block == 0:
            bits = all_ids[:, 0, :]
        third, sums = list_sums(layer_block, pair, w_edge, keys_row, list_of, start, stop)
        home, atoms = atom_round(layer_block, sums, w_atom, atoms, bits)
        message = fetch(message, third, keys_col, home, owner, first, last)
    return message, atoms


def solution(mesh):
    split = P(("rep", "edge"), None)
    whole = P(None, None, None)
    return jax.shard_map(
        on_device,
        mesh=mesh,
        in_specs=(split, split, whole, whole, split, split, split, split, split, P("rep")),
        out_specs=(split, split),
        check_vma=False,
    )
```

```python
import functools

import jax
import jax.numpy as jnp
from jax import lax
from jax.experimental import pallas as pl
from jax.experimental.pallas import tpu as pltpu
from jax.sharding import PartitionSpec as P

ABLK = 128
BLOCKS = 2
AB_DEV = 2
SIDE = 4
PEERS = SIDE * SIDE * SIDE
STRIDES = (16, 4, 1)
GROUP_AXES = ((0, 1, 2), (1, 2, 0), (2, 0, 1))
GROUP_ROWS = ((0, 176), (176, 176), (352, 160))
MESH = pl.DeviceIdType.MESH
F32 = jnp.float32
BF16 = jnp.bfloat16


def silu(v):
    half = 0.5 * v
    return half + half * jnp.tanh(half)


def to_column(rows, column):
    turned = jnp.transpose(rows[...])
    for t in range(16):
        column[t * 128 : (t + 1) * 128, :] = turned[:, t : t + 1]


def coords(me):
    return [(me // s) % SIDE for s in STRIDES]


def moved(me, place, axis, step):
    new = (place[axis] + step) % SIDE
    return me + (new - place[axis]) * STRIDES[axis], new


def peer_at(me, i, sign):
    i0, i1, i2 = i % 4, (i // 4) % 4, i // 16
    dx, dz, dy = i0, i1 + i0, i2 + i1 + i0
    px = (me // 16 + sign * dx + 16) % 4
    pz = ((me // 4) % 4 + sign * dz + 16) % 4
    py = (me % 4 + sign * dy + 16) % 4
    return px * 16 + pz * 4 + py


def exchange_kernel(
    layer_block,
    msg,
    w_hbm,
    order_rows,
    place_rows,
    ids,
    paired,
    ids_out,
    order,
    places,
    weights,
    second,
    outgoing,
    arrived,
    total,
    w_sem,
    send_sem,
    recv_sem,
    id_send,
    id_recv,
):
    me = lax.axis_index("edge")
    rep = lax.axis_index("rep")
    place = coords(me)
    barrier = pltpu.get_barrier_semaphore()

    def greet(i, carry):
        pl.semaphore_signal(barrier, inc=1, device_id=(peer_at(me, i, 1), rep), device_id_type=MESH)
        return carry

    lax.fori_loop(1, PEERS, greet, 0)
    if layer_block == 0:

        @pl.when(rep == 1)
        def _():
            pl.delay(25000)

    load = pltpu.make_async_copy(w_hbm.at[pl.ds(3 * layer_block, 2)], weights, w_sem)
    load.start()
    to_column(order_rows, order)
    to_column(place_rows, places)
    load.wait()

    def dense(c, carry):
        rows = pl.ds(pl.multiple_of(c * 256, 256), 256)
        first = silu(jnp.dot(msg[rows, :], weights[0], preferred_element_type=F32)).astype(BF16)
        value = silu(jnp.dot(first, weights[1], preferred_element_type=F32)).astype(BF16)
        second[rows, :] = value
        return carry

    lax.fori_loop(0, 8, dense, 0)
    pl.semaphore_wait(barrier, PEERS - 1)

    id_copies = []
    for axis in range(3):
        ids_out[pl.ds(axis * SIDE + place[axis], 1)] = ids[...][None]
        for step in range(1, SIDE):
            peer, _ = moved(me, place, axis, step)
            copy = pltpu.make_async_remote_copy(
                src_ref=ids,
                dst_ref=ids_out.at[axis * SIDE + place[axis]],
                send_sem=id_send.at[axis * 3 + step - 1],
                recv_sem=id_recv.at[axis * 3 + step - 1],
                device_id=(peer, rep),
                device_id_type=MESH,
            )
            copy.start()
            id_copies.append(copy)

    def message(i):
        return pltpu.make_async_remote_copy(
            src_ref=outgoing.at[pl.ds(pl.multiple_of(i * 32, 32), 32)],
            dst_ref=arrived.at[pl.ds(pl.multiple_of(i * 32, 32), 32)],
            send_sem=send_sem.at[i],
            recv_sem=recv_sem.at[i],
            device_id=(peer_at(me, i, 1), rep),
            device_id_type=MESH,
        )

    def send_chunk(c, carry):
        wanted = jnp.concatenate(
            [
                order[pl.ds(pl.multiple_of(peer_at(me, c * 8 + j, 1) * 32, 32), 32), :]
                for j in range(8)
            ],
            axis=0,
        )
        pick = (wanted == lax.broadcasted_iota(jnp.int32, (256, 2048), 1)).astype(F32).astype(BF16)
        rows = jnp.dot(pick, second[...], preferred_element_type=F32).astype(BF16)
        outgoing[pl.ds(pl.multiple_of(c * 256, 256), 256), :] = rows

        def start(j, inner):
            message(c * 8 + j).start()
            return inner

        @pl.when(c == 0)
        def _():
            arrived[0:32, :] = rows[0:32, :]
            lax.fori_loop(1, 8, start, 0)

        @pl.when(c > 0)
        def _():
            lax.fori_loop(0, 8, start, 0)

        return carry

    lax.fori_loop(0, 8, send_chunk, 0)

    def take_chunk(c, carry):
        def arrive(j, inner):
            @pl.when(c * 8 + j > 0)
            def _():
                message(c * 8 + j).wait_recv()

            return inner

        lax.fori_loop(0, 8, arrive, 0)
        lane = lax.broadcasted_iota(jnp.int32, (1, 256), 1)
        source = peer_at(me, c * 8 + lane // 32, -1) * 32 + lane % 32
        block = arrived[pl.ds(pl.multiple_of(c * 256, 256), 256), :]

        def add(r, inner):
            rows = pl.ds(pl.multiple_of(r * 256, 256), 256)
            pick = (places[rows, :] == source).astype(F32).astype(BF16)
            value = jnp.dot(pick, block, preferred_element_type=F32)

            @pl.when(c == 0)
            def _():
                total[rows, :] = second[rows, :].astype(F32) + value

            @pl.when((c > 0) & (c < 7))
            def _():
                total[rows, :] += value

            @pl.when(c == 7)
            def _():
                paired[rows, :] = (total[rows, :] + value).astype(BF16)

            return inner

        lax.fori_loop(0, 8, add, 0)
        return carry

    lax.fori_loop(0, 8, take_chunk, 0)

    def finish(i, carry):
        message(i).wait_send()
        return carry

    lax.fori_loop(1, PEERS, finish, 0)
    for copy in id_copies:
        copy.wait()


def exchange(layer_block, message, w_edge, order, places, ids):
    rows, feat = message.shape
    vmem = pl.BlockSpec(memory_space=pltpu.VMEM)
    return pl.pallas_call(
        functools.partial(exchange_kernel, layer_block),
        out_shape=(
            jax.ShapeDtypeStruct((rows, feat), BF16),
            jax.ShapeDtypeStruct((3 * SIDE, 8, 128), jnp.int32),
        ),
        in_specs=[vmem, pl.BlockSpec(memory_space=pl.ANY), vmem, vmem, vmem],
        out_specs=(vmem, vmem),
        scratch_shapes=[
            pltpu.VMEM((rows, 1), jnp.int32),
            pltpu.VMEM((rows, 1), jnp.int32),
            pltpu.VMEM((2, feat, feat), BF16),
            pltpu.VMEM((rows, feat), BF16),
            pltpu.VMEM((rows, feat), BF16),
            pltpu.VMEM((rows, feat), BF16),
            pltpu.VMEM((rows, feat), F32),
            pltpu.SemaphoreType.DMA,
            pltpu.SemaphoreType.DMA((PEERS,)),
            pltpu.SemaphoreType.DMA((PEERS,)),
            pltpu.SemaphoreType.DMA((9,)),
            pltpu.SemaphoreType.DMA((9,)),
        ],
        name=f"exchange{layer_block}",
        compiler_params=pltpu.CompilerParams(collective_id=layer_block, has_side_effects=True),
    )(message, w_edge, order, places, ids)


def sums_kernel(layer_block, list_of, owner, start, pair, w_hbm, keys, third, out, weight, sums, zero, w_sem, sems):
    load = pltpu.make_async_copy(w_hbm.at[3 * layer_block + 2], weight, w_sem)
    load.start()
    zero[...] = jnp.zeros(zero.shape, BF16)

    def clear(d, carry):
        @pl.when(list_of[d] < 0)
        def _():
            pltpu.make_async_copy(zero, out.at[d], sems.at[d]).start()

        return carry

    lax.fori_loop(0, PEERS, clear, 0)
    load.wait()

    def dense(c, carry):
        rows = pl.ds(pl.multiple_of(c * 256, 256), 256)
        value = silu(jnp.dot(pair[rows, :], weight[...], preferred_element_type=F32))
        third[rows, :] = value.astype(BF16)
        return carry

    lax.fori_loop(0, 8, dense, 0)

    def one(l, carry):
        begin = jnp.minimum(start[l] // 128, 13)
        key = jnp.concatenate([keys[pl.ds(begin + t, 1), :] for t in range(3)], axis=1)
        want = l * ABLK + lax.broadcasted_iota(jnp.int32, (ABLK, 384), 0)
        pick = (key == want).astype(F32).astype(BF16)
        rows = third[pl.ds(pl.multiple_of(begin * 128, 128), 384), :]
        value = jnp.dot(pick, rows, preferred_element_type=F32).astype(BF16)
        for k in range(4):
            sums[l, k * 128 : (k + 1) * 128, :] = value[:, k * 128 : (k + 1) * 128]
        pltpu.make_async_copy(sums.at[l], out.at[owner[l]], sems.at[owner[l]]).start()
        return carry

    lax.fori_loop(0, owner.shape[0], one, 0, unroll=2)

    def finish(d, carry):
        pltpu.make_async_copy(zero, out.at[d], sems.at[d]).wait()
        return carry

    lax.fori_loop(0, PEERS, finish, 0)


def list_sums(layer_block, pair, w_edge, keys, list_of, owner, start):
    rows, feat = pair.shape
    vmem = pl.BlockSpec(memory_space=pltpu.VMEM)
    smem = pl.BlockSpec(memory_space=pltpu.SMEM)
    anywhere = pl.BlockSpec(memory_space=pl.ANY)
    return pl.pallas_call(
        functools.partial(sums_kernel, layer_block),
        out_shape=(
            jax.ShapeDtypeStruct((rows, feat), BF16),
            jax.ShapeDtypeStruct((PEERS, 512, 128), BF16),
        ),
        in_specs=[smem, smem, smem, vmem, anywhere, vmem],
        out_specs=(vmem, anywhere),
        scratch_shapes=[
            pltpu.VMEM((feat, feat), BF16),
            pltpu.VMEM((owner.shape[0], 512, 128), BF16),
            pltpu.VMEM((512, 128), BF16),
            pltpu.SemaphoreType.DMA,
            pltpu.SemaphoreType.DMA((PEERS,)),
        ],
        name=f"sums{layer_block}",
    )(list_of, owner, start, pair, w_edge, keys)


def atoms_kernel(layer_block, bits, sums, w_hbm, atoms, home, atoms_out, *scratch):
    names = ["r1", "t1", "r2", "t2", "r3", "fan", "sel"]
    bufs = {name: scratch[3 * n : 3 * n + 3] for n, name in enumerate(names)}
    flat, weight, w_sem, own_sem, s1, q1, s2, q2, s3, q3, s4, q4, s5, q5, s6, q6, out_sem = scratch[21:]
    me = lax.axis_index("edge")
    rep = lax.axis_index("rep")
    place = coords(me)
    barrier = pltpu.get_barrier_semaphore()
    for axis in range(3):
        for step in range(1, SIDE):
            peer, _ = moved(me, place, axis, step)
            pl.semaphore_signal(barrier, inc=1, device_id=(peer, rep), device_id_type=MESH)
    load = pltpu.make_async_copy(w_hbm.at[layer_block], weight, w_sem)
    load.start()

    def spot(g, va, vb, vc):
        index = [None] * 3
        for axis, value in zip(GROUP_AXES[g], (va, vb, vc)):
            index[axis] = value
        return tuple(index)

    def number(g, va, vb, vc):
        x, z, y = spot(g, va, vb, vc)
        return x * 16 + z * 4 + y

    def rows_of(g):
        return pl.ds(GROUP_ROWS[g][0], GROUP_ROWS[g][1])

    every = pl.ds(0, SIDE)
    send = pltpu.make_async_remote_copy
    here = [[place[axis] for axis in GROUP_AXES[g]] for g in range(3)]
    started = []

    own_copies = {}
    for j in range(SIDE):
        for g in range(3):
            ha, hb, hc = here[g]
            vb = (hb + 1 + j) % SIDE
            copy = pltpu.make_async_copy(
                sums.at[spot(g, ha, vb, every) + (rows_of(g),)], bufs["r1"][g].at[0, j], own_sem.at[g, j]
            )
            copy.start()
            own_copies[g, j] = copy
    pl.semaphore_wait(barrier, 9)

    in1 = {}
    for j in range(SIDE):
        for k in (2, 1, 3):
            for g in range(3):
                ha, hb, hc = here[g]
                peer, va = moved(me, place, GROUP_AXES[g][0], k)
                vb = (hb + 1 + j) % SIDE
                copy = send(
                    src_ref=sums.at[spot(g, va, vb, every) + (rows_of(g),)],
                    dst_ref=bufs["r1"][g].at[k, j],
                    send_sem=s1.at[g, k, j],
                    recv_sem=q1.at[g, k, j],
                    device_id=(peer, rep),
                    device_id_type=MESH,
                )
                copy.start()
                in1[g, k, j] = copy
                started.append(copy)

    in2 = {}
    for j in range(SIDE):
        for g in range(3):
            ha, hb, hc = here[g]
            n = GROUP_ROWS[g][1]
            axis_a = GROUP_AXES[g][0]
            vb = (hb + 1 + j) % SIDE
            own_copies[g, j].wait()
            for k in range(1, SIDE):
                in1[g, k, j].wait_recv()
            r1, t1 = bufs["r1"][g], bufs["t1"][g]

            def one(m, carry, g=g, j=j, ha=ha, hb=hb, hc=hc, vb=vb, axis_a=axis_a, r1=r1, t1=t1, n=n):
                dest = number(g, ha, vb, m)
                low = jnp.zeros((n, 128), F32)
                high = jnp.zeros((n, 128), F32)
                for k in range(SIDE):
                    source = (ha - k + SIDE) % SIDE
                    bit = bits[axis_a * SIDE + source, dest].astype(F32)
                    value = r1[k, j, m].astype(F32)
                    upper = value * bit
                    high = high + upper
                    low = low + (value - upper)
                t1[j, m, 0] = low.astype(BF16)
                t1[j, m, 1] = high.astype(BF16)
                return carry

            lax.fori_loop(0, SIDE, one, 0)
            if j < SIDE - 1:
                peer, _ = moved(me, place, GROUP_AXES[g][1], 1 + j)
                for i in range(SIDE):
                    vc = (hc + 1 + i) % SIDE
                    copy = send(
                        src_ref=t1.at[j, vc],
                        dst_ref=bufs["r2"][g].at[j, vc],
                        send_sem=s2.at[g, j, i],
                        recv_sem=q2.at[g, j, i],
                        device_id=(peer, rep),
                        device_id_type=MESH,
                    )
                    copy.start()
                    in2[g, j, i] = copy
                    started.append(copy)

    in3 = {}
    for i in range(SIDE):
        for g in range(3):
            ha, hb, hc = here[g]
            vc = (hc + 1 + i) % SIDE
            for j in range(SIDE - 1):
                in2[g, j, i].wait_recv()
            t1, r2, t2 = bufs["t1"][g], bufs["r2"][g], bufs["t2"][g]
            for slot in range(AB_DEV):
                value = t1[SIDE - 1, vc, slot].astype(F32)
                for j in range(SIDE - 1):
                    value = value + r2[j, vc, slot].astype(F32)
                t2[i, slot] = value.astype(BF16)
            if i < SIDE - 1:
                peer, _ = moved(me, place, GROUP_AXES[g][2], 1 + i)
                copy = send(
                    src_ref=t2.at[i],
                    dst_ref=bufs["r3"][g].at[i],
                    send_sem=s3.at[g, i],
                    recv_sem=q3.at[g, i],
                    device_id=(peer, rep),
                    device_id_type=MESH,
                )
                copy.start()
                in3[g, i] = copy
                started.append(copy)

    for g in range(3):
        for i in range(SIDE - 1):
            in3[g, i].wait_recv()
        t2, r3 = bufs["t2"][g], bufs["r3"][g]
        for slot in range(AB_DEV):
            value = t2[SIDE - 1, slot].astype(F32)
            for i in range(SIDE - 1):
                value = value + r3[i, slot].astype(F32)
            flat[slot, rows_of(g), :] = value.astype(BF16)

    load.wait()
    for slot in range(AB_DEV):
        gathered = jnp.concatenate([flat[slot, k * 128 : (k + 1) * 128, :] for k in range(4)], axis=1)
        update = silu(jnp.dot(gathered, weight[...], preferred_element_type=F32))
        rows = slice(slot * ABLK, (slot + 1) * ABLK)
        fresh = (atoms[rows, :].astype(F32) + update).astype(BF16)
        atoms_out[rows, :] = fresh
        for k in range(4):
            flat[slot, k * 128 : (k + 1) * 128, :] = fresh[:, k * 128 : (k + 1) * 128]
    in4 = {}
    for g in range(3):
        fan = bufs["fan"][g]
        fan[0, 0] = flat[:, rows_of(g), :]
        for k in (2, 1, 3):
            peer, _ = moved(me, place, GROUP_AXES[g][2], k)
            copy = send(
                src_ref=fan.at[0, 0],
                dst_ref=fan.at[0, k],
                send_sem=s4.at[g, k],
                recv_sem=q4.at[g, k],
                device_id=(peer, rep),
                device_id_type=MESH,
            )
            copy.start()
            in4[g, k] = copy
            started.append(copy)

    in5 = {}
    for i in (0, 1, 3, 2):
        for g in range(3):
            fan = bufs["fan"][g]
            if i:
                in4[g, i].wait_recv()
            for k in (2, 1, 3):
                peer, _ = moved(me, place, GROUP_AXES[g][1], k)
                copy = send(
                    src_ref=fan.at[0, i],
                    dst_ref=fan.at[k, i],
                    send_sem=s5.at[g, k, i],
                    recv_sem=q5.at[g, k, i],
                    device_id=(peer, rep),
                    device_id_type=MESH,
                )
                copy.start()
                in5[g, k, i] = copy
                started.append(copy)

    out_copies = []
    in6 = []
    for j in (0, 1, 3, 2):
        for g in range(3):
            ha, hb, hc = here[g]
            fan, sel = bufs["fan"][g], bufs["sel"][g]
            axis_a = GROUP_AXES[g][0]
            if j:
                for i in range(SIDE):
                    in5[g, j, i].wait_recv()
            vb = (hb - j + SIDE) % SIDE

            def choose(m, carry, g=g, j=j, ha=ha, hc=hc, vb=vb, axis_a=axis_a, fan=fan, sel=sel):
                vc = (hc - m + SIDE) % SIDE
                dest = number(g, ha, vb, vc)
                for k in range(SIDE):
                    bit = bits[axis_a * SIDE + (ha + k) % SIDE, dest]
                    sel[k, j, vc] = jnp.where(bit > 0, fan[j, m, 1], fan[j, m, 0])
                return carry

            lax.fori_loop(0, SIDE, choose, 0)
            target = home.at[spot(g, ha, vb, every) + (rows_of(g),)]
            for k in (2, 1, 3):
                peer, _ = moved(me, place, axis_a, k)
                copy = send(
                    src_ref=sel.at[k, j],
                    dst_ref=target,
                    send_sem=s6.at[g, k, j],
                    recv_sem=q6.at[g, k, j],
                    device_id=(peer, rep),
                    device_id_type=MESH,
                )
                copy.start()
                in6.append(copy)
                started.append(copy)
            copy = pltpu.make_async_copy(sel.at[0, j], target, out_sem.at[g, j])
            copy.start()
            out_copies.append(copy)

    for copy in out_copies:
        copy.wait()
    for copy in in6:
        copy.wait_recv()
    for copy in started:
        copy.wait_send()


def atom_round(layer_block, sums, w_atom, atoms, bits):
    feat = atoms.shape[1]
    vmem = pl.BlockSpec(memory_space=pltpu.VMEM)
    anywhere = pl.BlockSpec(memory_space=pl.ANY)

    def per_group(*lead):
        return [pltpu.VMEM(lead + (n, 128), BF16) for _, n in GROUP_ROWS]

    dma = pltpu.SemaphoreType.DMA
    scratch = (
        per_group(4, 4, 4)
        + per_group(4, 4, 2)
        + per_group(3, 4, 2)
        + per_group(4, 2)
        + per_group(3, 2)
        + per_group(4, 4, 2)
        + per_group(4, 4, 4)
        + [
            pltpu.VMEM((2, 512, 128), BF16),
            pltpu.VMEM((feat, feat), BF16),
            dma,
            dma((3, 4)),
            dma((3, 4, 4)),
            dma((3, 4, 4)),
            dma((3, 3, 4)),
            dma((3, 3, 4)),
            dma((3, 3)),
            dma((3, 3)),
            dma((3, 4)),
            dma((3, 4)),
            dma((3, 4, 4)),
            dma((3, 4, 4)),
            dma((3, 4, 4)),
            dma((3, 4, 4)),
            dma((3, 4)),
        ]
    )
    home, fresh = pl.pallas_call(
        functools.partial(atoms_kernel, layer_block),
        out_shape=(
            jax.ShapeDtypeStruct((SIDE, SIDE, SIDE, 512, 128), BF16),
            jax.ShapeDtypeStruct(atoms.shape, BF16),
        ),
        in_specs=[pl.BlockSpec(memory_space=pltpu.SMEM), anywhere, anywhere, vmem],
        out_specs=(anywhere, vmem),
        scratch_shapes=scratch,
        name=f"atoms{layer_block}",
        compiler_params=pltpu.CompilerParams(
            collective_id=BLOCKS + layer_block, has_side_effects=True, vmem_limit_bytes=56 << 20
        ),
    )(bits, sums.reshape(SIDE, SIDE, SIDE, 512, 128), w_atom, atoms)
    return home.reshape(PEERS, 512, 128), fresh


def fetch_kernel(owner, first, last, msg, third, keys, home, out, column, blocks, acc, ready, sems):
    count = owner.shape[0]
    step = pl.program_id(0)

    def copy(l):
        return pltpu.make_async_copy(home.at[owner[l]], blocks.at[l], sems.at[l])

    @pl.when(step == 0)
    def _():
        def begin(l, carry):
            copy(l).start()
            return carry

        lax.fori_loop(0, count, begin, 0)
        ready[0] = 0
        to_column(keys, column)

    def finish(l, carry):
        copy(l).wait()
        return carry

    final = step * 4 + 3
    needed = jnp.where(step == 3, count, jnp.minimum(last[final] + 4, count))
    lax.fori_loop(ready[0], needed, finish, 0)
    ready[0] = needed

    for t in range(4):
        tile = step * 4 + t
        rows = pl.ds(t * 128, 128)
        low = first[tile]

        def part(base):
            want = base * ABLK + lax.broadcasted_iota(jnp.int32, (128, 512), 1)
            key = column[pl.ds(pl.multiple_of(tile * 128, 128), 128), :]
            pick = (key == want).astype(F32).astype(BF16)
            at = [jnp.minimum(base + j, count - 1) for j in range(4)]
            block = jnp.concatenate(
                [
                    jnp.concatenate([blocks[at[j], k * 128 : (k + 1) * 128, :] for k in range(4)], axis=1)
                    for j in range(4)
                ],
                axis=0,
            )
            return jnp.dot(pick, block, preferred_element_type=F32)

        base = msg[rows, :].astype(F32) + third[rows, :].astype(F32)
        found = part(low)
        out[rows, :] = (base + found).astype(BF16)

        @pl.when(last[tile] >= low + 4)
        def _():
            acc[...] = msg[rows, :].astype(F32) + third[rows, :].astype(F32) + part(low)

            def more(i, carry):
                acc[...] += part(low + 4 * i)
                return carry

            lax.fori_loop(1, (last[tile] - low) // 4 + 1, more, 0)
            out[rows, :] = acc[...].astype(BF16)


def fetch(message, third, keys, home, owner, first, last):
    rows, feat = message.shape
    lists = owner.shape[0]
    block = pl.BlockSpec((512, feat), lambda i, *_: (i, 0))
    return pl.pallas_call(
        fetch_kernel,
        out_shape=jax.ShapeDtypeStruct((rows, feat), BF16),
        grid_spec=pltpu.PrefetchScalarGridSpec(
            num_scalar_prefetch=3,
            grid=(rows // 512,),
            in_specs=[
                block,
                block,
                pl.BlockSpec((16, 128), lambda i, *_: (0, 0)),
                pl.BlockSpec(memory_space=pl.ANY),
            ],
            out_specs=block,
            scratch_shapes=[
                pltpu.VMEM((rows, 1), jnp.int32),
                pltpu.VMEM((lists, 512, 128), BF16),
                pltpu.VMEM((128, feat), F32),
                pltpu.SMEM((1,), jnp.int32),
                pltpu.SemaphoreType.DMA((lists,)),
            ],
        ),
        name="fetch",
        compiler_params=pltpu.CompilerParams(dimension_semantics=("arbitrary",)),
    )(owner, first, last, message, third, keys, home)


def on_device(
    edge_feats,
    atom_feats,
    w_edge,
    w_atom,
    send_order,
    recv_pos,
    edge_list,
    edge_atom,
    list_block,
    block_home,
):
    lists = list_block.shape[1]
    list_table = jnp.arange(lists, dtype=jnp.int32)
    peer_table = jnp.arange(PEERS, dtype=jnp.int32)
    block_table = jnp.arange(block_home.shape[0], dtype=jnp.int32)
    list_place = jnp.sum(
        jnp.where(list_block[0][:, None] == block_table[None, :], block_home[None, :], 0), axis=1
    )
    owner = list_place // AB_DEV
    placing = owner[None, :] == peer_table[:, None]
    list_of = jnp.max(jnp.where(placing, list_table[None, :], -1), axis=1)
    slot_of = jnp.sum(jnp.where(placing, (list_place % AB_DEV)[None, :], 0), axis=1)
    edge_lists = edge_list[0]
    start = jnp.sum((edge_lists[None, :] < list_table[:, None]).astype(jnp.int32), axis=1)
    tiled_lists = edge_lists.reshape(16, 128)
    first, last = tiled_lists[:, 0], tiled_lists[:, 127]
    keys = edge_lists * ABLK + edge_atom[0]
    keys = keys.reshape(16, 128)
    order = send_order.reshape(16, 128)
    places = recv_pos.reshape(16, 128)
    ids = jnp.broadcast_to(jnp.pad(slot_of, (0, 128 - PEERS))[None, :], (8, 128))
    message, atoms = edge_feats, atom_feats
    for layer_block in range(BLOCKS):
        pair, all_ids = exchange(layer_block, message, w_edge, order, places, ids)
        if layer_block == 0:
            bits = all_ids[:, 0, :]
        third, sums = list_sums(layer_block, pair, w_edge, keys, list_of, owner, start)
        home, atoms = atom_round(layer_block, sums, w_atom, atoms, bits)
        message = fetch(message, third, keys, home, owner, first, last)
    return message, atoms


def solution(mesh):
    split = P(("rep", "edge"), None)
    whole = P(None, None, None)
    return jax.shard_map(
        on_device,
        mesh=mesh,
        in_specs=(split, split, whole, whole, split, split, split, split, split, P("rep")),
        out_specs=(split, split),
        check_vma=False,
    )
```

```python
import functools

import jax
import jax.numpy as jnp
from jax import lax
from jax.experimental import pallas as pl
from jax.experimental.pallas import tpu as pltpu
from jax.sharding import PartitionSpec as P

ABLK = 128
BLOCKS = 2
AB_DEV = 2
SIDE = 4
PEERS = SIDE * SIDE * SIDE
STRIDES = (16, 4, 1)
GROUP_AXES = ((0, 1, 2), (1, 2, 0), (2, 0, 1))
GROUP_ROWS = ((0, 176), (176, 176), (352, 160))
MESH = pl.DeviceIdType.MESH
F32 = jnp.float32
BF16 = jnp.bfloat16
STAGGER = 25000
DENSE_ROWS = 256


def silu(v):
    half = 0.5 * v
    return half + half * jnp.tanh(half)


def to_column(rows, column):
    turned = jnp.transpose(rows[...])
    for t in range(16):
        column[t * 128 : (t + 1) * 128, :] = turned[:, t : t + 1]


def coords(me):
    return [(me // s) % SIDE for s in STRIDES]


def moved(me, place, axis, step):
    new = (place[axis] + step) % SIDE
    return me + (new - place[axis]) * STRIDES[axis], new


def peer_at(me, i, sign):
    i0, i1, i2 = i % 4, (i // 4) % 4, i // 16
    dx, dz, dy = i0, i1 + i0, i2 + i1 + i0
    px = (me // 16 + sign * dx + 16) % 4
    pz = ((me // 4) % 4 + sign * dz + 16) % 4
    py = (me % 4 + sign * dy + 16) % 4
    return px * 16 + pz * 4 + py


def exchange_kernel(
    layer_block,
    msg,
    w_hbm,
    order,
    places,
    ids,
    paired,
    ids_out,
    weights,
    tall,
    outgoing,
    arrived,
    w_sem,
    send_sem,
    recv_sem,
    id_send,
    id_recv,
):
    me = lax.axis_index("edge")
    rep = lax.axis_index("rep")
    place = coords(me)
    barrier = pltpu.get_barrier_semaphore()
    load = pltpu.make_async_copy(w_hbm.at[pl.ds(3 * layer_block, 2)], weights, w_sem)
    load.start()

    def greet(i, carry):
        pl.semaphore_signal(barrier, inc=1, device_id=(peer_at(me, i, 1), rep), device_id_type=MESH)
        return carry

    lax.fori_loop(1, PEERS, greet, 0)
    if layer_block == 0:

        @pl.when(rep == 1)
        def _():
            pl.delay(STAGGER)

    load.wait()

    def dense(c, carry):
        rows = pl.ds(pl.multiple_of(c * DENSE_ROWS, DENSE_ROWS), DENSE_ROWS)
        first = silu(jnp.dot(msg[rows, :], weights[0], preferred_element_type=F32)).astype(BF16)
        value = silu(jnp.dot(first, weights[1], preferred_element_type=F32)).astype(BF16).astype(F32)
        for k in range(4):
            tall[rows, k, :] = value[:, k * 128 : (k + 1) * 128]
        return carry

    lax.fori_loop(0, msg.shape[0] // DENSE_ROWS, dense, 0)
    pl.semaphore_wait(barrier, PEERS - 1)

    id_copies = []
    for axis in range(3):
        ids_out[pl.ds(axis * SIDE + place[axis], 1)] = ids[...][None]
        for step in range(1, SIDE):
            peer, _ = moved(me, place, axis, step)
            copy = pltpu.make_async_remote_copy(
                src_ref=ids,
                dst_ref=ids_out.at[axis * SIDE + place[axis]],
                send_sem=id_send.at[axis * 3 + step - 1],
                recv_sem=id_recv.at[axis * 3 + step - 1],
                device_id=(peer, rep),
                device_id_type=MESH,
            )
            copy.start()
            id_copies.append(copy)

    def message(i, source):
        return pltpu.make_async_remote_copy(
            src_ref=outgoing.at[pl.ds(i * 32, 32)],
            dst_ref=arrived.at[pl.ds(source * 32, 32)],
            send_sem=send_sem.at[i],
            recv_sem=recv_sem.at[i],
            device_id=(peer_at(me, i, 1), rep),
            device_id_type=MESH,
        )

    def row_of(t):
        return tall[order[t]].astype(BF16)

    for k in range(32):
        arrived[me * 32 + k] = row_of(me * 32 + k)

    def send_one(i, carry):
        peer = peer_at(me, i, 1)
        for k in range(32):
            outgoing[i * 32 + k] = row_of(peer * 32 + k)
        message(i, me).start()
        return carry

    lax.fori_loop(1, PEERS, send_one, 0)

    def arrive(i, carry):
        message(i, peer_at(me, i, -1)).wait_recv()
        return carry

    lax.fori_loop(1, PEERS, arrive, 0)

    def add(c, carry):
        for k in range(32):
            row = c * 32 + k
            tall[row] = tall[row] + arrived[places[row]].astype(F32)
        rows = pl.ds(pl.multiple_of(c * 32, 32), 32)
        for k in range(4):
            paired[rows, k * 128 : (k + 1) * 128] = tall[rows, k, :].astype(BF16)
        return carry

    lax.fori_loop(0, PEERS, add, 0)

    def finish(i, carry):
        message(i, me).wait_send()
        return carry

    lax.fori_loop(1, PEERS, finish, 0)
    for copy in id_copies:
        copy.wait()


def exchange(layer_block, message, w_edge, order, places, ids):
    rows, feat = message.shape
    vmem = pl.BlockSpec(memory_space=pltpu.VMEM)
    smem = pl.BlockSpec(memory_space=pltpu.SMEM)
    return pl.pallas_call(
        functools.partial(exchange_kernel, layer_block),
        out_shape=(
            jax.ShapeDtypeStruct((rows, feat), BF16),
            jax.ShapeDtypeStruct((3 * SIDE, 8, 128), jnp.int32),
        ),
        in_specs=[vmem, pl.BlockSpec(memory_space=pl.ANY), smem, smem, vmem],
        out_specs=(vmem, vmem),
        scratch_shapes=[
            pltpu.VMEM((2, feat, feat), BF16),
            pltpu.VMEM((rows, 4, 128), F32),
            pltpu.VMEM((rows, 4, 128), BF16),
            pltpu.VMEM((rows, 4, 128), BF16),
            pltpu.SemaphoreType.DMA,
            pltpu.SemaphoreType.DMA((PEERS,)),
            pltpu.SemaphoreType.DMA((PEERS,)),
            pltpu.SemaphoreType.DMA((9,)),
            pltpu.SemaphoreType.DMA((9,)),
        ],
        name=f"exchange{layer_block}",
        compiler_params=pltpu.CompilerParams(collective_id=layer_block, has_side_effects=True),
    )(message, w_edge, order, places, ids)


def sums_kernel(layer_block, list_of, owner, start, pair, w_hbm, keys, third, out, weight, sums, zero, w_sem, sems):
    load = pltpu.make_async_copy(w_hbm.at[3 * layer_block + 2], weight, w_sem)
    load.start()
    zero[...] = jnp.zeros(zero.shape, BF16)

    def clear(d, carry):
        @pl.when(list_of[d] < 0)
        def _():
            pltpu.make_async_copy(zero, out.at[d], sems.at[d]).start()

        return carry

    lax.fori_loop(0, PEERS, clear, 0)
    load.wait()

    def dense(c, carry):
        rows = pl.ds(pl.multiple_of(c * 256, 256), 256)
        value = silu(jnp.dot(pair[rows, :], weight[...], preferred_element_type=F32))
        third[rows, :] = value.astype(BF16)
        return carry

    lax.fori_loop(0, 8, dense, 0)

    def one(l, carry):
        begin = jnp.minimum(start[l] // 128, 13)
        key = jnp.concatenate([keys[pl.ds(begin + t, 1), :] for t in range(3)], axis=1)
        want = l * ABLK + lax.broadcasted_iota(jnp.int32, (ABLK, 384), 0)
        pick = (key == want).astype(F32).astype(BF16)
        rows = third[pl.ds(pl.multiple_of(begin * 128, 128), 384), :]
        value = jnp.dot(pick, rows, preferred_element_type=F32).astype(BF16)
        for k in range(4):
            sums[l, k * 128 : (k + 1) * 128, :] = value[:, k * 128 : (k + 1) * 128]
        pltpu.make_async_copy(sums.at[l], out.at[owner[l]], sems.at[owner[l]]).start()
        return carry

    lax.fori_loop(0, owner.shape[0], one, 0, unroll=2)

    def finish(d, carry):
        pltpu.make_async_copy(zero, out.at[d], sems.at[d]).wait()
        return carry

    lax.fori_loop(0, PEERS, finish, 0)


def list_sums(layer_block, pair, w_edge, keys, list_of, owner, start):
    rows, feat = pair.shape
    vmem = pl.BlockSpec(memory_space=pltpu.VMEM)
    smem = pl.BlockSpec(memory_space=pltpu.SMEM)
    anywhere = pl.BlockSpec(memory_space=pl.ANY)
    return pl.pallas_call(
        functools.partial(sums_kernel, layer_block),
        out_shape=(
            jax.ShapeDtypeStruct((rows, feat), BF16),
            jax.ShapeDtypeStruct((PEERS, 512, 128), BF16),
        ),
        in_specs=[smem, smem, smem, vmem, anywhere, vmem],
        out_specs=(vmem, anywhere),
        scratch_shapes=[
            pltpu.VMEM((feat, feat), BF16),
            pltpu.VMEM((owner.shape[0], 512, 128), BF16),
            pltpu.VMEM((512, 128), BF16),
            pltpu.SemaphoreType.DMA,
            pltpu.SemaphoreType.DMA((PEERS,)),
        ],
        name=f"sums{layer_block}",
    )(list_of, owner, start, pair, w_edge, keys)


def atoms_kernel(layer_block, bits, sums, w_hbm, atoms, home, atoms_out, *scratch):
    names = ["r1", "t1", "r2", "t2", "r3", "fan", "sel"]
    bufs = {name: scratch[3 * n : 3 * n + 3] for n, name in enumerate(names)}
    flat, weight, w_sem, own_sem, s1, q1, s2, q2, s3, q3, s4, q4, s5, q5, s6, q6, out_sem = scratch[21:]
    me = lax.axis_index("edge")
    rep = lax.axis_index("rep")
    place = coords(me)
    barrier = pltpu.get_barrier_semaphore()
    for axis in range(3):
        for step in range(1, SIDE):
            peer, _ = moved(me, place, axis, step)
            pl.semaphore_signal(barrier, inc=1, device_id=(peer, rep), device_id_type=MESH)
    load = pltpu.make_async_copy(w_hbm.at[layer_block], weight, w_sem)
    load.start()

    def spot(g, va, vb, vc):
        index = [None] * 3
        for axis, value in zip(GROUP_AXES[g], (va, vb, vc)):
            index[axis] = value
        return tuple(index)

    def number(g, va, vb, vc):
        x, z, y = spot(g, va, vb, vc)
        return x * 16 + z * 4 + y

    def rows_of(g):
        return pl.ds(GROUP_ROWS[g][0], GROUP_ROWS[g][1])

    every = pl.ds(0, SIDE)
    send = pltpu.make_async_remote_copy
    here = [[place[axis] for axis in GROUP_AXES[g]] for g in range(3)]
    started = []

    own_copies = {}
    for j in range(SIDE):
        for g in range(3):
            ha, hb, hc = here[g]
            vb = (hb + 1 + j) % SIDE
            copy = pltpu.make_async_copy(
                sums.at[spot(g, ha, vb, every) + (rows_of(g),)], bufs["r1"][g].at[0, j], own_sem.at[g, j]
            )
            copy.start()
            own_copies[g, j] = copy
    pl.semaphore_wait(barrier, 9)

    in1 = {}
    for j in range(SIDE):
        for k in (2, 1, 3):
            for g in range(3):
                ha, hb, hc = here[g]
                peer, va = moved(me, place, GROUP_AXES[g][0], k)
                vb = (hb + 1 + j) % SIDE
                copy = send(
                    src_ref=sums.at[spot(g, va, vb, every) + (rows_of(g),)],
                    dst_ref=bufs["r1"][g].at[k, j],
                    send_sem=s1.at[g, k, j],
                    recv_sem=q1.at[g, k, j],
                    device_id=(peer, rep),
                    device_id_type=MESH,
                )
                copy.start()
                in1[g, k, j] = copy
                started.append(copy)

    in2 = {}
    for j in range(SIDE):
        for g in range(3):
            ha, hb, hc = here[g]
            n = GROUP_ROWS[g][1]
            axis_a = GROUP_AXES[g][0]
            vb = (hb + 1 + j) % SIDE
            own_copies[g, j].wait()
            for k in range(1, SIDE):
                in1[g, k, j].wait_recv()
            r1, t1 = bufs["r1"][g], bufs["t1"][g]

            def one(m, carry, g=g, j=j, ha=ha, hb=hb, hc=hc, vb=vb, axis_a=axis_a, r1=r1, t1=t1, n=n):
                dest = number(g, ha, vb, m)
                low = jnp.zeros((n, 128), F32)
                high = jnp.zeros((n, 128), F32)
                for k in range(SIDE):
                    source = (ha - k + SIDE) % SIDE
                    bit = bits[axis_a * SIDE + source, dest].astype(F32)
                    value = r1[k, j, m].astype(F32)
                    upper = value * bit
                    high = high + upper
                    low = low + (value - upper)
                t1[j, m, 0] = low.astype(BF16)
                t1[j, m, 1] = high.astype(BF16)
                return carry

            lax.fori_loop(0, SIDE, one, 0)
            if j < SIDE - 1:
                peer, _ = moved(me, place, GROUP_AXES[g][1], 1 + j)
                for i in range(SIDE):
                    vc = (hc + 1 + i) % SIDE
                    copy = send(
                        src_ref=t1.at[j, vc],
                        dst_ref=bufs["r2"][g].at[j, vc],
                        send_sem=s2.at[g, j, i],
                        recv_sem=q2.at[g, j, i],
                        device_id=(peer, rep),
                        device_id_type=MESH,
                    )
                    copy.start()
                    in2[g, j, i] = copy
                    started.append(copy)

    in3 = {}
    for i in range(SIDE):
        for g in range(3):
            ha, hb, hc = here[g]
            vc = (hc + 1 + i) % SIDE
            for j in range(SIDE - 1):
                in2[g, j, i].wait_recv()
            t1, r2, t2 = bufs["t1"][g], bufs["r2"][g], bufs["t2"][g]
            for slot in range(AB_DEV):
                value = t1[SIDE - 1, vc, slot].astype(F32)
                for j in range(SIDE - 1):
                    value = value + r2[j, vc, slot].astype(F32)
                t2[i, slot] = value.astype(BF16)
            if i < SIDE - 1:
                peer, _ = moved(me, place, GROUP_AXES[g][2], 1 + i)
                copy = send(
                    src_ref=t2.at[i],
                    dst_ref=bufs["r3"][g].at[i],
                    send_sem=s3.at[g, i],
                    recv_sem=q3.at[g, i],
                    device_id=(peer, rep),
                    device_id_type=MESH,
                )
                copy.start()
                in3[g, i] = copy
                started.append(copy)

    for g in range(3):
        for i in range(SIDE - 1):
            in3[g, i].wait_recv()
        t2, r3 = bufs["t2"][g], bufs["r3"][g]
        for slot in range(AB_DEV):
            value = t2[SIDE - 1, slot].astype(F32)
            for i in range(SIDE - 1):
                value = value + r3[i, slot].astype(F32)
            flat[slot, rows_of(g), :] = value.astype(BF16)

    load.wait()
    for slot in range(AB_DEV):
        gathered = jnp.concatenate([flat[slot, k * 128 : (k + 1) * 128, :] for k in range(4)], axis=1)
        update = silu(jnp.dot(gathered, weight[...], preferred_element_type=F32))
        rows = slice(slot * ABLK, (slot + 1) * ABLK)
        fresh = (atoms[rows, :].astype(F32) + update).astype(BF16)
        atoms_out[rows, :] = fresh
        for k in range(4):
            flat[slot, k * 128 : (k + 1) * 128, :] = fresh[:, k * 128 : (k + 1) * 128]
    in4 = {}
    for g in range(3):
        fan = bufs["fan"][g]
        fan[0, 0] = flat[:, rows_of(g), :]
        for k in (2, 1, 3):
            peer, _ = moved(me, place, GROUP_AXES[g][2], k)
            copy = send(
                src_ref=fan.at[0, 0],
                dst_ref=fan.at[0, k],
                send_sem=s4.at[g, k],
                recv_sem=q4.at[g, k],
                device_id=(peer, rep),
                device_id_type=MESH,
            )
            copy.start()
            in4[g, k] = copy
            started.append(copy)

    in5 = {}
    for i in (0, 1, 3, 2):
        for g in range(3):
            fan = bufs["fan"][g]
            if i:
                in4[g, i].wait_recv()
            for k in (2, 1, 3):
                peer, _ = moved(me, place, GROUP_AXES[g][1], k)
                copy = send(
                    src_ref=fan.at[0, i],
                    dst_ref=fan.at[k, i],
                    send_sem=s5.at[g, k, i],
                    recv_sem=q5.at[g, k, i],
                    device_id=(peer, rep),
                    device_id_type=MESH,
                )
                copy.start()
                in5[g, k, i] = copy
                started.append(copy)

    out_copies = []
    in6 = []
    for j in (0, 1, 3, 2):
        for g in range(3):
            ha, hb, hc = here[g]
            fan, sel = bufs["fan"][g], bufs["sel"][g]
            axis_a = GROUP_AXES[g][0]
            if j:
                for i in range(SIDE):
                    in5[g, j, i].wait_recv()
            vb = (hb - j + SIDE) % SIDE

            def choose(m, carry, g=g, j=j, ha=ha, hc=hc, vb=vb, axis_a=axis_a, fan=fan, sel=sel):
                vc = (hc - m + SIDE) % SIDE
                dest = number(g, ha, vb, vc)
                for k in range(SIDE):
                    bit = bits[axis_a * SIDE + (ha + k) % SIDE, dest]
                    sel[k, j, vc] = jnp.where(bit > 0, fan[j, m, 1], fan[j, m, 0])
                return carry

            lax.fori_loop(0, SIDE, choose, 0)
            target = home.at[spot(g, ha, vb, every) + (rows_of(g),)]
            for k in (2, 1, 3):
                peer, _ = moved(me, place, axis_a, k)
                copy = send(
                    src_ref=sel.at[k, j],
                    dst_ref=target,
                    send_sem=s6.at[g, k, j],
                    recv_sem=q6.at[g, k, j],
                    device_id=(peer, rep),
                    device_id_type=MESH,
                )
                copy.start()
                in6.append(copy)
                started.append(copy)
            copy = pltpu.make_async_copy(sel.at[0, j], target, out_sem.at[g, j])
            copy.start()
            out_copies.append(copy)

    for copy in out_copies:
        copy.wait()
    for copy in in6:
        copy.wait_recv()
    for copy in started:
        copy.wait_send()


def atom_round(layer_block, sums, w_atom, atoms, bits):
    feat = atoms.shape[1]
    vmem = pl.BlockSpec(memory_space=pltpu.VMEM)
    anywhere = pl.BlockSpec(memory_space=pl.ANY)

    def per_group(*lead):
        return [pltpu.VMEM(lead + (n, 128), BF16) for _, n in GROUP_ROWS]

    dma = pltpu.SemaphoreType.DMA
    scratch = (
        per_group(4, 4, 4)
        + per_group(4, 4, 2)
        + per_group(3, 4, 2)
        + per_group(4, 2)
        + per_group(3, 2)
        + per_group(4, 4, 2)
        + per_group(4, 4, 4)
        + [
            pltpu.VMEM((2, 512, 128), BF16),
            pltpu.VMEM((feat, feat), BF16),
            dma,
            dma((3, 4)),
            dma((3, 4, 4)),
            dma((3, 4, 4)),
            dma((3, 3, 4)),
            dma((3, 3, 4)),
            dma((3, 3)),
            dma((3, 3)),
            dma((3, 4)),
            dma((3, 4)),
            dma((3, 4, 4)),
            dma((3, 4, 4)),
            dma((3, 4, 4)),
            dma((3, 4, 4)),
            dma((3, 4)),
        ]
    )
    home, fresh = pl.pallas_call(
        functools.partial(atoms_kernel, layer_block),
        out_shape=(
            jax.ShapeDtypeStruct((SIDE, SIDE, SIDE, 512, 128), BF16),
            jax.ShapeDtypeStruct(atoms.shape, BF16),
        ),
        in_specs=[pl.BlockSpec(memory_space=pltpu.SMEM), anywhere, anywhere, vmem],
        out_specs=(anywhere, vmem),
        scratch_shapes=scratch,
        name=f"atoms{layer_block}",
        compiler_params=pltpu.CompilerParams(
            collective_id=BLOCKS + layer_block, has_side_effects=True, vmem_limit_bytes=56 << 20
        ),
    )(bits, sums.reshape(SIDE, SIDE, SIDE, 512, 128), w_atom, atoms)
    return home.reshape(PEERS, 512, 128), fresh


def fetch_kernel(owner, first, last, msg, third, keys, home, out, column, blocks, acc, ready, sems):
    count = owner.shape[0]
    step = pl.program_id(0)

    def copy(l):
        return pltpu.make_async_copy(home.at[owner[l]], blocks.at[l], sems.at[l])

    @pl.when(step == 0)
    def _():
        def begin(l, carry):
            copy(l).start()
            return carry

        lax.fori_loop(0, count, begin, 0)
        ready[0] = 0
        to_column(keys, column)

    def finish(l, carry):
        copy(l).wait()
        return carry

    final = step * 4 + 3
    needed = jnp.where(step == 3, count, jnp.minimum(last[final] + 4, count))
    lax.fori_loop(ready[0], needed, finish, 0)
    ready[0] = needed

    for t in range(4):
        tile = step * 4 + t
        rows = pl.ds(t * 128, 128)
        low = first[tile]

        def part(base):
            want = base * ABLK + lax.broadcasted_iota(jnp.int32, (128, 512), 1)
            key = column[pl.ds(pl.multiple_of(tile * 128, 128), 128), :]
            pick = (key == want).astype(F32).astype(BF16)
            at = [jnp.minimum(base + j, count - 1) for j in range(4)]
            block = jnp.concatenate(
                [
                    jnp.concatenate([blocks[at[j], k * 128 : (k + 1) * 128, :] for k in range(4)], axis=1)
                    for j in range(4)
                ],
                axis=0,
            )
            return jnp.dot(pick, block, preferred_element_type=F32)

        base = msg[rows, :].astype(F32) + third[rows, :].astype(F32)
        found = part(low)
        out[rows, :] = (base + found).astype(BF16)

        @pl.when(last[tile] >= low + 4)
        def _():
            acc[...] = msg[rows, :].astype(F32) + third[rows, :].astype(F32) + part(low)

            def more(i, carry):
                acc[...] += part(low + 4 * i)
                return carry

            lax.fori_loop(1, (last[tile] - low) // 4 + 1, more, 0)
            out[rows, :] = acc[...].astype(BF16)


def fetch(message, third, keys, home, owner, first, last):
    rows, feat = message.shape
    lists = owner.shape[0]
    block = pl.BlockSpec((512, feat), lambda i, *_: (i, 0))
    return pl.pallas_call(
        fetch_kernel,
        out_shape=jax.ShapeDtypeStruct((rows, feat), BF16),
        grid_spec=pltpu.PrefetchScalarGridSpec(
            num_scalar_prefetch=3,
            grid=(rows // 512,),
            in_specs=[
                block,
                block,
                pl.BlockSpec((16, 128), lambda i, *_: (0, 0)),
                pl.BlockSpec(memory_space=pl.ANY),
            ],
            out_specs=block,
            scratch_shapes=[
                pltpu.VMEM((rows, 1), jnp.int32),
                pltpu.VMEM((lists, 512, 128), BF16),
                pltpu.VMEM((128, feat), F32),
                pltpu.SMEM((1,), jnp.int32),
                pltpu.SemaphoreType.DMA((lists,)),
            ],
        ),
        name="fetch",
        compiler_params=pltpu.CompilerParams(dimension_semantics=("arbitrary",)),
    )(owner, first, last, message, third, keys, home)


def on_device(
    edge_feats,
    atom_feats,
    w_edge,
    w_atom,
    send_order,
    recv_pos,
    edge_list,
    edge_atom,
    list_block,
    block_home,
):
    lists = list_block.shape[1]
    list_table = jnp.arange(lists, dtype=jnp.int32)
    peer_table = jnp.arange(PEERS, dtype=jnp.int32)
    block_table = jnp.arange(block_home.shape[0], dtype=jnp.int32)
    list_place = jnp.sum(
        jnp.where(list_block[0][:, None] == block_table[None, :], block_home[None, :], 0), axis=1
    )
    owner = list_place // AB_DEV
    placing = owner[None, :] == peer_table[:, None]
    list_of = jnp.max(jnp.where(placing, list_table[None, :], -1), axis=1)
    slot_of = jnp.sum(jnp.where(placing, (list_place % AB_DEV)[None, :], 0), axis=1)
    edge_lists = edge_list[0]
    start = jnp.sum((edge_lists[None, :] < list_table[:, None]).astype(jnp.int32), axis=1)
    tiled_lists = edge_lists.reshape(16, 128)
    first, last = tiled_lists[:, 0], tiled_lists[:, 127]
    keys = edge_lists * ABLK + edge_atom[0]
    keys = keys.reshape(16, 128)
    order = send_order.reshape(-1)
    places = recv_pos.reshape(-1)
    ids = jnp.broadcast_to(jnp.pad(slot_of, (0, 128 - PEERS))[None, :], (8, 128))
    message, atoms = edge_feats, atom_feats
    for layer_block in range(BLOCKS):
        pair, all_ids = exchange(layer_block, message, w_edge, order, places, ids)
        if layer_block == 0:
            bits = all_ids[:, 0, :]
        third, sums = list_sums(layer_block, pair, w_edge, keys, list_of, owner, start)
        home, atoms = atom_round(layer_block, sums, w_atom, atoms, bits)
        message = fetch(message, third, keys, home, owner, first, last)
    return message, atoms


def solution(mesh):
    split = P(("rep", "edge"), None)
    whole = P(None, None, None)
    return jax.shard_map(
        on_device,
        mesh=mesh,
        in_specs=(split, split, whole, whole, split, split, split, split, split, P("rep")),
        out_specs=(split, split),
        check_vma=False,
    )
```

```python
import functools

import jax
import jax.numpy as jnp
from jax import lax
from jax.experimental import pallas as pl
from jax.experimental.pallas import tpu as pltpu
from jax.sharding import PartitionSpec as P

ABLK = 128
BLOCKS = 2
AB_DEV = 2
SIDE = 4
PEERS = SIDE * SIDE * SIDE
STRIDES = (16, 4, 1)
GROUP_AXES = ((0, 1, 2), (1, 2, 0), (2, 0, 1))
GROUP_ROWS = ((0, 176), (176, 176), (352, 160))
MESH = pl.DeviceIdType.MESH
F32 = jnp.float32
BF16 = jnp.bfloat16
STAGGER = 26000
DENSE_ROWS = 256


def silu(v):
    half = 0.5 * v
    return half + half * jnp.tanh(half)


def to_column(rows, column):
    turned = jnp.transpose(rows[...])
    for t in range(16):
        column[t * 128 : (t + 1) * 128, :] = turned[:, t : t + 1]


def coords(me):
    return [(me // s) % SIDE for s in STRIDES]


def moved(me, place, axis, step):
    new = (place[axis] + step) % SIDE
    return me + (new - place[axis]) * STRIDES[axis], new


def peer_at(me, i, sign):
    i0, i1, i2 = i % 4, (i // 4) % 4, i // 16
    dx, dz, dy = i0, i1 + i0, i2 + i1 + i0
    px = (me // 16 + sign * dx + 16) % 4
    pz = ((me // 4) % 4 + sign * dz + 16) % 4
    py = (me % 4 + sign * dy + 16) % 4
    return px * 16 + pz * 4 + py


def exchange_kernel(
    layer_block,
    msg,
    w_hbm,
    order,
    places,
    ids,
    paired,
    ids_out,
    weights,
    tall,
    outgoing,
    arrived,
    w_sem,
    send_sem,
    recv_sem,
    id_send,
    id_recv,
):
    me = lax.axis_index("edge")
    rep = lax.axis_index("rep")
    place = coords(me)
    barrier = pltpu.get_barrier_semaphore()
    load = pltpu.make_async_copy(w_hbm.at[pl.ds(3 * layer_block, 2)], weights, w_sem)
    load.start()

    def greet(i, carry):
        peer = me + i
        peer = jnp.where(peer >= PEERS, peer - PEERS, peer)
        pl.semaphore_signal(barrier, inc=1, device_id=(peer, rep), device_id_type=MESH)
        return carry

    lax.fori_loop(1, PEERS, greet, 0)
    if layer_block == 0:

        @pl.when(rep == 1)
        def _():
            pl.delay(STAGGER)

    load.wait()

    def dense(c, carry):
        rows = pl.ds(pl.multiple_of(c * DENSE_ROWS, DENSE_ROWS), DENSE_ROWS)
        first = silu(jnp.dot(msg[rows, :], weights[0], preferred_element_type=F32)).astype(BF16)
        value = silu(jnp.dot(first, weights[1], preferred_element_type=F32)).astype(BF16).astype(F32)
        tall[rows] = value.reshape(DENSE_ROWS, 4, 128)
        return carry

    lax.fori_loop(0, msg.shape[0] // DENSE_ROWS, dense, 0)
    pl.semaphore_wait(barrier, PEERS - 1)

    id_copies = []
    for axis in range(3):
        ids_out[pl.ds(axis * SIDE + place[axis], 1)] = ids[...][None]
        for step in range(1, SIDE):
            peer, _ = moved(me, place, axis, step)
            copy = pltpu.make_async_remote_copy(
                src_ref=ids,
                dst_ref=ids_out.at[axis * SIDE + place[axis]],
                send_sem=id_send.at[axis * 3 + step - 1],
                recv_sem=id_recv.at[axis * 3 + step - 1],
                device_id=(peer, rep),
                device_id_type=MESH,
            )
            copy.start()
            id_copies.append(copy)

    def message(i, source):
        return pltpu.make_async_remote_copy(
            src_ref=outgoing.at[pl.ds(i * 32, 32)],
            dst_ref=arrived.at[pl.ds(source * 32, 32)],
            send_sem=send_sem.at[i],
            recv_sem=recv_sem.at[i],
            device_id=(peer_at(me, i, 1), rep),
            device_id_type=MESH,
        )

    def row_of(t):
        return tall[order[t]].astype(BF16)

    for k in range(32):
        arrived[me * 32 + k] = row_of(me * 32 + k)

    def send_one(i, carry):
        peer = peer_at(me, i, 1)
        for k in range(32):
            outgoing[i * 32 + k] = row_of(peer * 32 + k)
        message(i, me).start()
        return carry

    lax.fori_loop(1, PEERS, send_one, 0)

    def arrive(i, carry):
        message(i, peer_at(me, i, -1)).wait_recv()
        return carry

    lax.fori_loop(1, PEERS, arrive, 0)

    def add(c, carry):
        for k in range(32):
            row = c * 32 + k
            tall[row] = tall[row] + arrived[places[row]].astype(F32)
        rows = pl.ds(pl.multiple_of(c * 32, 32), 32)
        paired[rows, :] = tall[rows].reshape(32, 4 * 128).astype(BF16)
        return carry

    lax.fori_loop(0, PEERS, add, 0)

    def finish(i, carry):
        message(i, me).wait_send()
        return carry

    lax.fori_loop(1, PEERS, finish, 0)
    for copy in id_copies:
        copy.wait()


def exchange(layer_block, message, w_edge, order, places, ids):
    rows, feat = message.shape
    vmem = pl.BlockSpec(memory_space=pltpu.VMEM)
    smem = pl.BlockSpec(memory_space=pltpu.SMEM)
    return pl.pallas_call(
        functools.partial(exchange_kernel, layer_block),
        out_shape=(
            jax.ShapeDtypeStruct((rows, feat), BF16),
            jax.ShapeDtypeStruct((3 * SIDE, 8, 128), jnp.int32),
        ),
        in_specs=[vmem, pl.BlockSpec(memory_space=pl.ANY), smem, smem, vmem],
        out_specs=(vmem, vmem),
        scratch_shapes=[
            pltpu.VMEM((2, feat, feat), BF16),
            pltpu.VMEM((rows, 4, 128), F32),
            pltpu.VMEM((rows, 4, 128), BF16),
            pltpu.VMEM((rows, 4, 128), BF16),
            pltpu.SemaphoreType.DMA,
            pltpu.SemaphoreType.DMA((PEERS,)),
            pltpu.SemaphoreType.DMA((PEERS,)),
            pltpu.SemaphoreType.DMA((9,)),
            pltpu.SemaphoreType.DMA((9,)),
        ],
        name=f"exchange{layer_block}",
        compiler_params=pltpu.CompilerParams(collective_id=layer_block, has_side_effects=True),
    )(message, w_edge, order, places, ids)


def sums_kernel(layer_block, list_of, owner, start, pair, w_hbm, keys, third, out, weight, sums, zero, w_sem, sems):
    load = pltpu.make_async_copy(w_hbm.at[3 * layer_block + 2], weight, w_sem)
    load.start()
    zero[...] = jnp.zeros(zero.shape, BF16)

    def clear(d, carry):
        @pl.when(list_of[d] < 0)
        def _():
            pltpu.make_async_copy(zero, out.at[d], sems.at[d]).start()

        return carry

    lax.fori_loop(0, PEERS, clear, 0)
    load.wait()

    def dense(c, carry):
        rows = pl.ds(pl.multiple_of(c * 256, 256), 256)
        value = silu(jnp.dot(pair[rows, :], weight[...], preferred_element_type=F32))
        third[rows, :] = value.astype(BF16)
        return carry

    lax.fori_loop(0, 8, dense, 0)

    def one(l, carry):
        begin = jnp.minimum(start[l] // 128, 13)
        key = jnp.concatenate([keys[pl.ds(begin + t, 1), :] for t in range(3)], axis=1)
        want = l * ABLK + lax.broadcasted_iota(jnp.int32, (ABLK, 384), 0)
        pick = (key == want).astype(F32).astype(BF16)
        rows = third[pl.ds(pl.multiple_of(begin * 128, 128), 384), :]
        value = jnp.dot(pick, rows, preferred_element_type=F32).astype(BF16)
        for k in range(4):
            sums[l, k * 128 : (k + 1) * 128, :] = value[:, k * 128 : (k + 1) * 128]
        pltpu.make_async_copy(sums.at[l], out.at[owner[l]], sems.at[owner[l]]).start()
        return carry

    lax.fori_loop(0, owner.shape[0], one, 0, unroll=2)

    def finish(d, carry):
        pltpu.make_async_copy(zero, out.at[d], sems.at[d]).wait()
        return carry

    lax.fori_loop(0, PEERS, finish, 0)


def list_sums(layer_block, pair, w_edge, keys, list_of, owner, start):
    rows, feat = pair.shape
    vmem = pl.BlockSpec(memory_space=pltpu.VMEM)
    smem = pl.BlockSpec(memory_space=pltpu.SMEM)
    anywhere = pl.BlockSpec(memory_space=pl.ANY)
    return pl.pallas_call(
        functools.partial(sums_kernel, layer_block),
        out_shape=(
            jax.ShapeDtypeStruct((rows, feat), BF16),
            jax.ShapeDtypeStruct((PEERS, 512, 128), BF16),
        ),
        in_specs=[smem, smem, smem, vmem, anywhere, vmem],
        out_specs=(vmem, anywhere),
        scratch_shapes=[
            pltpu.VMEM((feat, feat), BF16),
            pltpu.VMEM((owner.shape[0], 512, 128), BF16),
            pltpu.VMEM((512, 128), BF16),
            pltpu.SemaphoreType.DMA,
            pltpu.SemaphoreType.DMA((PEERS,)),
        ],
        name=f"sums{layer_block}",
    )(list_of, owner, start, pair, w_edge, keys)


def atoms_kernel(layer_block, bits, sums, w_hbm, atoms, home, atoms_out, *scratch):
    names = ["r1", "t1", "r2", "t2", "r3", "fan", "sel"]
    bufs = {name: scratch[3 * n : 3 * n + 3] for n, name in enumerate(names)}
    flat, weight, w_sem, own_sem, s1, q1, s2, q2, s3, q3, s4, q4, s5, q5, s6, q6, out_sem = scratch[21:]
    me = lax.axis_index("edge")
    rep = lax.axis_index("rep")
    place = coords(me)
    barrier = pltpu.get_barrier_semaphore()
    for axis in range(3):
        for step in range(1, SIDE):
            peer, _ = moved(me, place, axis, step)
            pl.semaphore_signal(barrier, inc=1, device_id=(peer, rep), device_id_type=MESH)
    load = pltpu.make_async_copy(w_hbm.at[layer_block], weight, w_sem)
    load.start()

    def spot(g, va, vb, vc):
        index = [None] * 3
        for axis, value in zip(GROUP_AXES[g], (va, vb, vc)):
            index[axis] = value
        return tuple(index)

    def number(g, va, vb, vc):
        x, z, y = spot(g, va, vb, vc)
        return x * 16 + z * 4 + y

    def rows_of(g):
        return pl.ds(GROUP_ROWS[g][0], GROUP_ROWS[g][1])

    every = pl.ds(0, SIDE)
    send = pltpu.make_async_remote_copy
    here = [[place[axis] for axis in GROUP_AXES[g]] for g in range(3)]
    started = []

    own_copies = {}
    for j in range(SIDE):
        for g in range(3):
            ha, hb, hc = here[g]
            vb = (hb + 1 + j) % SIDE
            copy = pltpu.make_async_copy(
                sums.at[spot(g, ha, vb, every) + (rows_of(g),)], bufs["r1"][g].at[0, j], own_sem.at[g, j]
            )
            copy.start()
            own_copies[g, j] = copy
    pl.semaphore_wait(barrier, 9)

    in1 = {}
    for j in range(SIDE):
        for k in (2, 1, 3):
            for g in range(3):
                ha, hb, hc = here[g]
                peer, va = moved(me, place, GROUP_AXES[g][0], k)
                vb = (hb + 1 + j) % SIDE
                copy = send(
                    src_ref=sums.at[spot(g, va, vb, every) + (rows_of(g),)],
                    dst_ref=bufs["r1"][g].at[k, j],
                    send_sem=s1.at[g, k, j],
                    recv_sem=q1.at[g, k, j],
                    device_id=(peer, rep),
                    device_id_type=MESH,
                )
                copy.start()
                in1[g, k, j] = copy
                started.append(copy)

    in2 = {}
    for j in range(SIDE):
        for g in range(3):
            ha, hb, hc = here[g]
            n = GROUP_ROWS[g][1]
            axis_a = GROUP_AXES[g][0]
            vb = (hb + 1 + j) % SIDE
            own_copies[g, j].wait()
            for k in range(1, SIDE):
                in1[g, k, j].wait_recv()
            r1, t1 = bufs["r1"][g], bufs["t1"][g]

            def one(m, carry, g=g, j=j, ha=ha, hb=hb, hc=hc, vb=vb, axis_a=axis_a, r1=r1, t1=t1, n=n):
                dest = number(g, ha, vb, m)
                low = jnp.zeros((n, 128), F32)
                high = jnp.zeros((n, 128), F32)
                for k in range(SIDE):
                    source = (ha - k + SIDE) % SIDE
                    bit = bits[axis_a * SIDE + source, dest].astype(F32)
                    value = r1[k, j, m].astype(F32)
                    upper = value * bit
                    high = high + upper
                    low = low + (value - upper)
                t1[j, m, 0] = low.astype(BF16)
                t1[j, m, 1] = high.astype(BF16)
                return carry

            lax.fori_loop(0, SIDE, one, 0)
            if j < SIDE - 1:
                peer, _ = moved(me, place, GROUP_AXES[g][1], 1 + j)
                for i in range(SIDE):
                    vc = (hc + 1 + i) % SIDE
                    copy = send(
                        src_ref=t1.at[j, vc],
                        dst_ref=bufs["r2"][g].at[j, vc],
                        send_sem=s2.at[g, j, i],
                        recv_sem=q2.at[g, j, i],
                        device_id=(peer, rep),
                        device_id_type=MESH,
                    )
                    copy.start()
                    in2[g, j, i] = copy
                    started.append(copy)

    in3 = {}
    for i in range(SIDE):
        for g in range(3):
            ha, hb, hc = here[g]
            vc = (hc + 1 + i) % SIDE
            for j in range(SIDE - 1):
                in2[g, j, i].wait_recv()
            t1, r2, t2 = bufs["t1"][g], bufs["r2"][g], bufs["t2"][g]
            for slot in range(AB_DEV):
                value = t1[SIDE - 1, vc, slot].astype(F32)
                for j in range(SIDE - 1):
                    value = value + r2[j, vc, slot].astype(F32)
                t2[i, slot] = value.astype(BF16)
            if i < SIDE - 1:
                peer, _ = moved(me, place, GROUP_AXES[g][2], 1 + i)
                copy = send(
                    src_ref=t2.at[i],
                    dst_ref=bufs["r3"][g].at[i],
                    send_sem=s3.at[g, i],
                    recv_sem=q3.at[g, i],
                    device_id=(peer, rep),
                    device_id_type=MESH,
                )
                copy.start()
                in3[g, i] = copy
                started.append(copy)

    for g in range(3):
        for i in range(SIDE - 1):
            in3[g, i].wait_recv()
        t2, r3 = bufs["t2"][g], bufs["r3"][g]
        for slot in range(AB_DEV):
            value = t2[SIDE - 1, slot].astype(F32)
            for i in range(SIDE - 1):
                value = value + r3[i, slot].astype(F32)
            flat[slot, rows_of(g), :] = value.astype(BF16)

    load.wait()
    for slot in range(AB_DEV):
        gathered = jnp.concatenate([flat[slot, k * 128 : (k + 1) * 128, :] for k in range(4)], axis=1)
        update = silu(jnp.dot(gathered, weight[...], preferred_element_type=F32))
        rows = slice(slot * ABLK, (slot + 1) * ABLK)
        fresh = (atoms[rows, :].astype(F32) + update).astype(BF16)
        atoms_out[rows, :] = fresh
        for k in range(4):
            flat[slot, k * 128 : (k + 1) * 128, :] = fresh[:, k * 128 : (k + 1) * 128]
    in4 = {}
    for g in range(3):
        fan = bufs["fan"][g]
        fan[0, 0] = flat[:, rows_of(g), :]
        for k in (2, 1, 3):
            peer, _ = moved(me, place, GROUP_AXES[g][2], k)
            copy = send(
                src_ref=fan.at[0, 0],
                dst_ref=fan.at[0, k],
                send_sem=s4.at[g, k],
                recv_sem=q4.at[g, k],
                device_id=(peer, rep),
                device_id_type=MESH,
            )
            copy.start()
            in4[g, k] = copy
            started.append(copy)

    in5 = {}
    for i in (0, 1, 3, 2):
        for g in range(3):
            fan = bufs["fan"][g]
            if i:
                in4[g, i].wait_recv()
            for k in (2, 1, 3):
                peer, _ = moved(me, place, GROUP_AXES[g][1], k)
                copy = send(
                    src_ref=fan.at[0, i],
                    dst_ref=fan.at[k, i],
                    send_sem=s5.at[g, k, i],
                    recv_sem=q5.at[g, k, i],
                    device_id=(peer, rep),
                    device_id_type=MESH,
                )
                copy.start()
                in5[g, k, i] = copy
                started.append(copy)

    out_copies = []
    in6 = []
    for j in (0, 1, 3, 2):
        for g in range(3):
            ha, hb, hc = here[g]
            fan, sel = bufs["fan"][g], bufs["sel"][g]
            axis_a = GROUP_AXES[g][0]
            if j:
                for i in range(SIDE):
                    in5[g, j, i].wait_recv()
            vb = (hb - j + SIDE) % SIDE

            def choose(m, carry, g=g, j=j, ha=ha, hc=hc, vb=vb, axis_a=axis_a, fan=fan, sel=sel):
                vc = (hc - m + SIDE) % SIDE
                dest = number(g, ha, vb, vc)
                for k in range(SIDE):
                    bit = bits[axis_a * SIDE + (ha + k) % SIDE, dest]
                    sel[k, j, vc] = jnp.where(bit > 0, fan[j, m, 1], fan[j, m, 0])
                return carry

            lax.fori_loop(0, SIDE, choose, 0)
            target = home.at[spot(g, ha, vb, every) + (rows_of(g),)]
            for k in (2, 1, 3):
                peer, _ = moved(me, place, axis_a, k)
                copy = send(
                    src_ref=sel.at[k, j],
                    dst_ref=target,
                    send_sem=s6.at[g, k, j],
                    recv_sem=q6.at[g, k, j],
                    device_id=(peer, rep),
                    device_id_type=MESH,
                )
                copy.start()
                in6.append(copy)
                started.append(copy)
            copy = pltpu.make_async_copy(sel.at[0, j], target, out_sem.at[g, j])
            copy.start()
            out_copies.append(copy)

    for copy in out_copies:
        copy.wait()
    for copy in in6:
        copy.wait_recv()
    for copy in started:
        copy.wait_send()


def atom_round(layer_block, sums, w_atom, atoms, bits):
    feat = atoms.shape[1]
    vmem = pl.BlockSpec(memory_space=pltpu.VMEM)
    anywhere = pl.BlockSpec(memory_space=pl.ANY)

    def per_group(*lead):
        return [pltpu.VMEM(lead + (n, 128), BF16) for _, n in GROUP_ROWS]

    dma = pltpu.SemaphoreType.DMA
    scratch = (
        per_group(4, 4, 4)
        + per_group(4, 4, 2)
        + per_group(3, 4, 2)
        + per_group(4, 2)
        + per_group(3, 2)
        + per_group(4, 4, 2)
        + per_group(4, 4, 4)
        + [
            pltpu.VMEM((2, 512, 128), BF16),
            pltpu.VMEM((feat, feat), BF16),
            dma,
            dma((3, 4)),
            dma((3, 4, 4)),
            dma((3, 4, 4)),
            dma((3, 3, 4)),
            dma((3, 3, 4)),
            dma((3, 3)),
            dma((3, 3)),
            dma((3, 4)),
            dma((3, 4)),
            dma((3, 4, 4)),
            dma((3, 4, 4)),
            dma((3, 4, 4)),
            dma((3, 4, 4)),
            dma((3, 4)),
        ]
    )
    home, fresh = pl.pallas_call(
        functools.partial(atoms_kernel, layer_block),
        out_shape=(
            jax.ShapeDtypeStruct((SIDE, SIDE, SIDE, 512, 128), BF16),
            jax.ShapeDtypeStruct(atoms.shape, BF16),
        ),
        in_specs=[pl.BlockSpec(memory_space=pltpu.SMEM), anywhere, anywhere, vmem],
        out_specs=(anywhere, vmem),
        scratch_shapes=scratch,
        name=f"atoms{layer_block}",
        compiler_params=pltpu.CompilerParams(
            collective_id=BLOCKS + layer_block, has_side_effects=True, vmem_limit_bytes=56 << 20
        ),
    )(bits, sums.reshape(SIDE, SIDE, SIDE, 512, 128), w_atom, atoms)
    return home.reshape(PEERS, 512, 128), fresh


def fetch_kernel(owner, first, last, msg, third, keys, home, out, column, blocks, acc, ready, sems):
    count = owner.shape[0]
    step = pl.program_id(0)

    def copy(l):
        return pltpu.make_async_copy(home.at[owner[l]], blocks.at[l], sems.at[l])

    @pl.when(step == 0)
    def _():
        def begin(l, carry):
            copy(l).start()
            return carry

        lax.fori_loop(0, count, begin, 0)
        ready[0] = 0
        to_column(keys, column)

    def finish(l, carry):
        copy(l).wait()
        return carry

    final = step * 4 + 3
    needed = jnp.where(step == 3, count, jnp.minimum(last[final] + 4, count))
    lax.fori_loop(ready[0], needed, finish, 0)
    ready[0] = needed

    for t in range(4):
        tile = step * 4 + t
        rows = pl.ds(t * 128, 128)
        low = first[tile]

        def part(base):
            want = base * ABLK + lax.broadcasted_iota(jnp.int32, (128, 512), 1)
            key = column[pl.ds(pl.multiple_of(tile * 128, 128), 128), :]
            pick = (key == want).astype(F32).astype(BF16)
            at = [jnp.minimum(base + j, count - 1) for j in range(4)]
            block = jnp.concatenate(
                [
                    jnp.concatenate([blocks[at[j], k * 128 : (k + 1) * 128, :] for k in range(4)], axis=1)
                    for j in range(4)
                ],
                axis=0,
            )
            return jnp.dot(pick, block, preferred_element_type=F32)

        base = msg[rows, :].astype(F32) + third[rows, :].astype(F32)
        found = part(low)
        out[rows, :] = (base + found).astype(BF16)

        @pl.when(last[tile] >= low + 4)
        def _():
            acc[...] = msg[rows, :].astype(F32) + third[rows, :].astype(F32) + part(low)

            def more(i, carry):
                acc[...] += part(low + 4 * i)
                return carry

            lax.fori_loop(1, (last[tile] - low) // 4 + 1, more, 0)
            out[rows, :] = acc[...].astype(BF16)


def fetch(message, third, keys, home, owner, first, last):
    rows, feat = message.shape
    lists = owner.shape[0]
    block = pl.BlockSpec((512, feat), lambda i, *_: (i, 0))
    return pl.pallas_call(
        fetch_kernel,
        out_shape=jax.ShapeDtypeStruct((rows, feat), BF16),
        grid_spec=pltpu.PrefetchScalarGridSpec(
            num_scalar_prefetch=3,
            grid=(rows // 512,),
            in_specs=[
                block,
                block,
                pl.BlockSpec((16, 128), lambda i, *_: (0, 0)),
                pl.BlockSpec(memory_space=pl.ANY),
            ],
            out_specs=block,
            scratch_shapes=[
                pltpu.VMEM((rows, 1), jnp.int32),
                pltpu.VMEM((lists, 512, 128), BF16),
                pltpu.VMEM((128, feat), F32),
                pltpu.SMEM((1,), jnp.int32),
                pltpu.SemaphoreType.DMA((lists,)),
            ],
        ),
        name="fetch",
        compiler_params=pltpu.CompilerParams(dimension_semantics=("arbitrary",)),
    )(owner, first, last, message, third, keys, home)


def on_device(
    edge_feats,
    atom_feats,
    w_edge,
    w_atom,
    send_order,
    recv_pos,
    edge_list,
    edge_atom,
    list_block,
    block_home,
):
    lists = list_block.shape[1]
    list_table = jnp.arange(lists, dtype=jnp.int32)
    peer_table = jnp.arange(PEERS, dtype=jnp.int32)
    block_table = jnp.arange(block_home.shape[0], dtype=jnp.int32)
    list_place = jnp.sum(
        jnp.where(list_block[0][:, None] == block_table[None, :], block_home[None, :], 0), axis=1
    )
    owner = list_place // AB_DEV
    placing = owner[None, :] == peer_table[:, None]
    list_of = jnp.max(jnp.where(placing, list_table[None, :], -1), axis=1)
    slot_of = jnp.sum(jnp.where(placing, (list_place % AB_DEV)[None, :], 0), axis=1)
    edge_lists = edge_list[0]
    start = jnp.sum((edge_lists[None, :] < list_table[:, None]).astype(jnp.int32), axis=1)
    tiled_lists = edge_lists.reshape(16, 128)
    first, last = tiled_lists[:, 0], tiled_lists[:, 127]
    keys = edge_lists * ABLK + edge_atom[0]
    keys = keys.reshape(16, 128)
    order = send_order.reshape(-1)
    places = recv_pos.reshape(-1)
    ids = jnp.broadcast_to(jnp.pad(slot_of, (0, 128 - PEERS))[None, :], (8, 128))
    message, atoms = edge_feats, atom_feats
    for layer_block in range(BLOCKS):
        pair, all_ids = exchange(layer_block, message, w_edge, order, places, ids)
        if layer_block == 0:
            bits = all_ids[:, 0, :]
        third, sums = list_sums(layer_block, pair, w_edge, keys, list_of, owner, start)
        home, atoms = atom_round(layer_block, sums, w_atom, atoms, bits)
        message = fetch(message, third, keys, home, owner, first, last)
    return message, atoms


def solution(mesh):
    split = P(("rep", "edge"), None)
    whole = P(None, None, None)
    return jax.shard_map(
        on_device,
        mesh=mesh,
        in_specs=(split, split, whole, whole, split, split, split, split, split, P("rep")),
        out_specs=(split, split),
        check_vma=False,
    )
```

```python
import functools

import jax
import jax.numpy as jnp
from jax import lax
from jax.experimental import pallas as pl
from jax.experimental.pallas import tpu as pltpu
from jax.sharding import PartitionSpec as P

ABLK = 128
BLOCKS = 2
AB_DEV = 2
SIDE = 4
PEERS = SIDE * SIDE * SIDE
STRIDES = (16, 4, 1)
GROUP_AXES = ((0, 1, 2), (1, 2, 0), (2, 0, 1))
GROUP_ROWS = ((0, 176), (176, 176), (352, 160))
MESH = pl.DeviceIdType.MESH
F32 = jnp.float32
BF16 = jnp.bfloat16
STAGGER = 26000
DENSE_ROWS = 256


def silu(v):
    half = 0.5 * v
    return half + half * jnp.tanh(half)


def to_column(rows, column):
    turned = jnp.transpose(rows[...])
    for t in range(16):
        column[t * 128 : (t + 1) * 128, :] = turned[:, t : t + 1]


def coords(me):
    return [(me // s) % SIDE for s in STRIDES]


def moved(me, place, axis, step):
    new = (place[axis] + step) % SIDE
    return me + (new - place[axis]) * STRIDES[axis], new


def peer_at(me, i, sign):
    i0, i1, i2 = i % 4, (i // 4) % 4, i // 16
    dx, dz, dy = i0, i1 + i0, i2 + i1 + i0
    px = (me // 16 + sign * dx + 16) % 4
    pz = ((me // 4) % 4 + sign * dz + 16) % 4
    py = (me % 4 + sign * dy + 16) % 4
    return px * 16 + pz * 4 + py


def exchange_kernel(
    layer_block,
    msg,
    w_hbm,
    order,
    places,
    ids,
    paired,
    ids_out,
    weights,
    tall,
    outgoing,
    arrived,
    w_sem,
    send_sem,
    recv_sem,
    id_send,
    id_recv,
):
    me = lax.axis_index("edge")
    rep = lax.axis_index("rep")
    place = coords(me)
    barrier = pltpu.get_barrier_semaphore()
    load = pltpu.make_async_copy(w_hbm.at[pl.ds(3 * layer_block, 2)], weights, w_sem)
    load.start()

    def greet(i, carry):
        peer = me + i
        peer = jnp.where(peer >= PEERS, peer - PEERS, peer)
        pl.semaphore_signal(barrier, inc=1, device_id=(peer, rep), device_id_type=MESH)
        return carry

    lax.fori_loop(1, PEERS, greet, 0)
    if layer_block == 0:

        @pl.when(rep == 1)
        def _():
            pl.delay(STAGGER)

    load.wait()

    def dense(c, carry):
        rows = pl.ds(pl.multiple_of(c * DENSE_ROWS, DENSE_ROWS), DENSE_ROWS)
        first = silu(jnp.dot(msg[rows, :], weights[0], preferred_element_type=F32)).astype(BF16)
        value = silu(jnp.dot(first, weights[1], preferred_element_type=F32)).astype(BF16).astype(F32)
        tall[rows] = value.reshape(DENSE_ROWS, 4, 128)
        return carry

    lax.fori_loop(0, msg.shape[0] // DENSE_ROWS, dense, 0)
    pl.semaphore_wait(barrier, PEERS - 1)

    id_copies = []
    for axis in range(3):
        ids_out[pl.ds(axis * SIDE + place[axis], 1)] = ids[...][None]
        for step in range(1, SIDE):
            peer, _ = moved(me, place, axis, step)
            copy = pltpu.make_async_remote_copy(
                src_ref=ids,
                dst_ref=ids_out.at[axis * SIDE + place[axis]],
                send_sem=id_send.at[axis * 3 + step - 1],
                recv_sem=id_recv.at[axis * 3 + step - 1],
                device_id=(peer, rep),
                device_id_type=MESH,
            )
            copy.start()
            id_copies.append(copy)

    def message(i, source):
        return pltpu.make_async_remote_copy(
            src_ref=outgoing.at[pl.ds(i * 32, 32)],
            dst_ref=arrived.at[pl.ds(source * 32, 32)],
            send_sem=send_sem.at[i],
            recv_sem=recv_sem.at[i],
            device_id=(peer_at(me, i, 1), rep),
            device_id_type=MESH,
        )

    def row_of(t):
        return tall[order[t]].astype(BF16)

    for k in range(32):
        arrived[me * 32 + k] = row_of(me * 32 + k)

    def send_one(i, carry):
        peer = peer_at(me, i, 1)
        for k in range(32):
            outgoing[i * 32 + k] = row_of(peer * 32 + k)
        message(i, me).start()
        return carry

    lax.fori_loop(1, PEERS, send_one, 0)

    def arrive(i, carry):
        message(i, peer_at(me, i, -1)).wait_recv()
        return carry

    lax.fori_loop(1, PEERS, arrive, 0)

    def add(c, carry):
        for k in range(32):
            row = c * 32 + k
            tall[row] = tall[row] + arrived[places[row]].astype(F32)
        rows = pl.ds(pl.multiple_of(c * 32, 32), 32)
        paired[rows, :] = tall[rows].reshape(32, 4 * 128).astype(BF16)
        return carry

    lax.fori_loop(0, PEERS, add, 0)

    def finish(i, carry):
        message(i, me).wait_send()
        return carry

    lax.fori_loop(1, PEERS, finish, 0)
    for copy in id_copies:
        copy.wait()


def exchange(layer_block, message, w_edge, order, places, ids):
    rows, feat = message.shape
    vmem = pl.BlockSpec(memory_space=pltpu.VMEM)
    smem = pl.BlockSpec(memory_space=pltpu.SMEM)
    return pl.pallas_call(
        functools.partial(exchange_kernel, layer_block),
        out_shape=(
            jax.ShapeDtypeStruct((rows, feat), BF16),
            jax.ShapeDtypeStruct((3 * SIDE, 8, 128), jnp.int32),
        ),
        in_specs=[vmem, pl.BlockSpec(memory_space=pl.ANY), smem, smem, vmem],
        out_specs=(vmem, vmem),
        scratch_shapes=[
            pltpu.VMEM((2, feat, feat), BF16),
            pltpu.VMEM((rows, 4, 128), F32),
            pltpu.VMEM((rows, 4, 128), BF16),
            pltpu.VMEM((rows, 4, 128), BF16),
            pltpu.SemaphoreType.DMA,
            pltpu.SemaphoreType.DMA((PEERS,)),
            pltpu.SemaphoreType.DMA((PEERS,)),
            pltpu.SemaphoreType.DMA((9,)),
            pltpu.SemaphoreType.DMA((9,)),
        ],
        name=f"exchange{layer_block}",
        compiler_params=pltpu.CompilerParams(collective_id=layer_block, has_side_effects=True),
    )(message, w_edge, order, places, ids)


def sums_kernel(layer_block, list_of, owner, start, pair, w_hbm, keys, third, out, weight, sums, zero, w_sem, sems):
    load = pltpu.make_async_copy(w_hbm.at[3 * layer_block + 2], weight, w_sem)
    load.start()
    zero[...] = jnp.zeros(zero.shape, BF16)

    def clear(d, carry):
        @pl.when(list_of[d] < 0)
        def _():
            pltpu.make_async_copy(zero, out.at[d], sems.at[d]).start()

        return carry

    lax.fori_loop(0, PEERS, clear, 0)
    load.wait()

    def dense(c, carry):
        rows = pl.ds(pl.multiple_of(c * 256, 256), 256)
        value = silu(jnp.dot(pair[rows, :], weight[...], preferred_element_type=F32))
        third[rows, :] = value.astype(BF16)
        return carry

    lax.fori_loop(0, 8, dense, 0)

    def one(l, carry):
        begin = jnp.minimum(start[l] // 128, 13)
        key = jnp.concatenate([keys[pl.ds(begin + t, 1), :] for t in range(3)], axis=1)
        want = l * ABLK + lax.broadcasted_iota(jnp.int32, (ABLK, 384), 0)
        pick = (key == want).astype(F32).astype(BF16)
        rows = third[pl.ds(pl.multiple_of(begin * 128, 128), 384), :]
        value = jnp.dot(pick, rows, preferred_element_type=F32).astype(BF16)
        for k in range(4):
            sums[l, k * 128 : (k + 1) * 128, :] = value[:, k * 128 : (k + 1) * 128]
        pltpu.make_async_copy(sums.at[l], out.at[owner[l]], sems.at[owner[l]]).start()
        return carry

    lax.fori_loop(0, owner.shape[0], one, 0, unroll=2)

    def finish(d, carry):
        pltpu.make_async_copy(zero, out.at[d], sems.at[d]).wait()
        return carry

    lax.fori_loop(0, PEERS, finish, 0)


def list_sums(layer_block, pair, w_edge, keys, list_of, owner, start):
    rows, feat = pair.shape
    vmem = pl.BlockSpec(memory_space=pltpu.VMEM)
    smem = pl.BlockSpec(memory_space=pltpu.SMEM)
    anywhere = pl.BlockSpec(memory_space=pl.ANY)
    return pl.pallas_call(
        functools.partial(sums_kernel, layer_block),
        out_shape=(
            jax.ShapeDtypeStruct((rows, feat), BF16),
            jax.ShapeDtypeStruct((PEERS, 512, 128), BF16),
        ),
        in_specs=[smem, smem, smem, vmem, anywhere, vmem],
        out_specs=(vmem, anywhere),
        scratch_shapes=[
            pltpu.VMEM((feat, feat), BF16),
            pltpu.VMEM((owner.shape[0], 512, 128), BF16),
            pltpu.VMEM((512, 128), BF16),
            pltpu.SemaphoreType.DMA,
            pltpu.SemaphoreType.DMA((PEERS,)),
        ],
        name=f"sums{layer_block}",
    )(list_of, owner, start, pair, w_edge, keys)


def atoms_kernel(layer_block, bits, sums, w_hbm, atoms, home, atoms_out, *scratch):
    names = ["r1", "t1", "r2", "t2", "r3", "fan", "sel"]
    bufs = {name: scratch[3 * n : 3 * n + 3] for n, name in enumerate(names)}
    flat, weight, w_sem, own_sem, s1, q1, s2, q2, s3, q3, s4, q4, s5, q5, s6, q6, out_sem = scratch[21:]
    me = lax.axis_index("edge")
    rep = lax.axis_index("rep")
    place = coords(me)
    barrier = pltpu.get_barrier_semaphore()
    for axis in range(3):
        for step in range(1, SIDE):
            peer, _ = moved(me, place, axis, step)
            pl.semaphore_signal(barrier, inc=1, device_id=(peer, rep), device_id_type=MESH)
    load = pltpu.make_async_copy(w_hbm.at[layer_block], weight, w_sem)
    load.start()

    def spot(g, va, vb, vc):
        index = [None] * 3
        for axis, value in zip(GROUP_AXES[g], (va, vb, vc)):
            index[axis] = value
        return tuple(index)

    def number(g, va, vb, vc):
        x, z, y = spot(g, va, vb, vc)
        return x * 16 + z * 4 + y

    def rows_of(g):
        return pl.ds(GROUP_ROWS[g][0], GROUP_ROWS[g][1])

    every = pl.ds(0, SIDE)
    send = pltpu.make_async_remote_copy
    here = [[place[axis] for axis in GROUP_AXES[g]] for g in range(3)]
    started = []

    own_copies = {}
    for j in range(SIDE):
        for g in range(3):
            ha, hb, hc = here[g]
            vb = (hb + 1 + j) % SIDE
            copy = pltpu.make_async_copy(
                sums.at[spot(g, ha, vb, every) + (rows_of(g),)], bufs["r1"][g].at[0, j], own_sem.at[g, j]
            )
            copy.start()
            own_copies[g, j] = copy
    pl.semaphore_wait(barrier, 9)

    in1 = {}
    for j in range(SIDE):
        for k in (2, 1, 3):
            for g in range(3):
                ha, hb, hc = here[g]
                peer, va = moved(me, place, GROUP_AXES[g][0], k)
                vb = (hb + 1 + j) % SIDE
                copy = send(
                    src_ref=sums.at[spot(g, va, vb, every) + (rows_of(g),)],
                    dst_ref=bufs["r1"][g].at[k, j],
                    send_sem=s1.at[g, k, j],
                    recv_sem=q1.at[g, k, j],
                    device_id=(peer, rep),
                    device_id_type=MESH,
                )
                copy.start()
                in1[g, k, j] = copy
                started.append(copy)

    in2 = {}
    for j in range(SIDE):
        for g in range(3):
            ha, hb, hc = here[g]
            n = GROUP_ROWS[g][1]
            axis_a = GROUP_AXES[g][0]
            vb = (hb + 1 + j) % SIDE
            own_copies[g, j].wait()
            for k in range(1, SIDE):
                in1[g, k, j].wait_recv()
            r1, t1 = bufs["r1"][g], bufs["t1"][g]

            def one(m, carry, g=g, j=j, ha=ha, hb=hb, hc=hc, vb=vb, axis_a=axis_a, r1=r1, t1=t1, n=n):
                dest = number(g, ha, vb, m)
                low = jnp.zeros((n, 128), F32)
                high = jnp.zeros((n, 128), F32)
                for k in range(SIDE):
                    source = (ha - k + SIDE) % SIDE
                    bit = bits[axis_a * SIDE + source, dest].astype(F32)
                    value = r1[k, j, m].astype(F32)
                    upper = value * bit
                    high = high + upper
                    low = low + (value - upper)
                t1[j, m, 0] = low.astype(BF16)
                t1[j, m, 1] = high.astype(BF16)
                return carry

            lax.fori_loop(0, SIDE, one, 0)
            if j < SIDE - 1:
                peer, _ = moved(me, place, GROUP_AXES[g][1], 1 + j)
                for i in range(SIDE):
                    vc = (hc + 1 + i) % SIDE
                    copy = send(
                        src_ref=t1.at[j, vc],
                        dst_ref=bufs["r2"][g].at[j, vc],
                        send_sem=s2.at[g, j, i],
                        recv_sem=q2.at[g, j, i],
                        device_id=(peer, rep),
                        device_id_type=MESH,
                    )
                    copy.start()
                    in2[g, j, i] = copy
                    started.append(copy)

    in3 = {}
    for i in range(SIDE):
        for g in range(3):
            ha, hb, hc = here[g]
            vc = (hc + 1 + i) % SIDE
            for j in range(SIDE - 1):
                in2[g, j, i].wait_recv()
            t1, r2, t2 = bufs["t1"][g], bufs["r2"][g], bufs["t2"][g]
            for slot in range(AB_DEV):
                value = t1[SIDE - 1, vc, slot].astype(F32)
                for j in range(SIDE - 1):
                    value = value + r2[j, vc, slot].astype(F32)
                t2[i, slot] = value.astype(BF16)
            if i < SIDE - 1:
                peer, _ = moved(me, place, GROUP_AXES[g][2], 1 + i)
                copy = send(
                    src_ref=t2.at[i],
                    dst_ref=bufs["r3"][g].at[i],
                    send_sem=s3.at[g, i],
                    recv_sem=q3.at[g, i],
                    device_id=(peer, rep),
                    device_id_type=MESH,
                )
                copy.start()
                in3[g, i] = copy
                started.append(copy)

    for g in range(3):
        for i in range(SIDE - 1):
            in3[g, i].wait_recv()
        t2, r3 = bufs["t2"][g], bufs["r3"][g]
        for slot in range(AB_DEV):
            value = t2[SIDE - 1, slot].astype(F32)
            for i in range(SIDE - 1):
                value = value + r3[i, slot].astype(F32)
            flat[slot, rows_of(g), :] = value.astype(BF16)

    load.wait()
    for slot in range(AB_DEV):
        gathered = jnp.concatenate([flat[slot, k * 128 : (k + 1) * 128, :] for k in range(4)], axis=1)
        update = silu(jnp.dot(gathered, weight[...], preferred_element_type=F32))
        rows = slice(slot * ABLK, (slot + 1) * ABLK)
        fresh = (atoms[rows, :].astype(F32) + update).astype(BF16)
        atoms_out[rows, :] = fresh
        for k in range(4):
            flat[slot, k * 128 : (k + 1) * 128, :] = fresh[:, k * 128 : (k + 1) * 128]
    in4 = {}

    def hop(g, axis_at, step, source, target, send_sem, recv_sem):
        peer, _ = moved(me, place, GROUP_AXES[g][axis_at], step)
        copy = send(
            src_ref=source,
            dst_ref=target,
            send_sem=send_sem,
            recv_sem=recv_sem,
            device_id=(peer, rep),
            device_id_type=MESH,
        )
        copy.start()
        started.append(copy)
        return copy

    def half(g, which):
        n = GROUP_ROWS[g][1]
        cut = (n // 32) * 16 + (n // 16) % 2 * 16
        return pl.ds(0, cut) if which == 0 else pl.ds(cut, n - cut)

    both = pl.ds(0, AB_DEV)
    for g in range(3):
        fan = bufs["fan"][g]
        fan[0, 0] = flat[:, rows_of(g), :]
        for k in (1, 3):
            in4[g, k] = hop(g, 2, k, fan.at[0, 0], fan.at[0, k], s4.at[g, k], q4.at[g, k])
    on4 = {}
    for g in range(3):
        fan = bufs["fan"][g]
        for which, k in enumerate((1, 3)):
            in4[g, k].wait_recv()
            rows = half(g, which)
            on4[g, which] = hop(
                g,
                2,
                k,
                fan.at[0, k, both, rows],
                fan.at[0, 2, both, rows],
                s4.at[g, 2 * which],
                q4.at[g, 2 * which],
            )

    in5 = {}
    for i in (0, 1, 3, 2):
        for g in range(3):
            fan = bufs["fan"][g]
            if i == 2:
                on4[g, 0].wait_recv()
                on4[g, 1].wait_recv()
            for k in (1, 3):
                in5[g, k, i] = hop(g, 1, k, fan.at[0, i], fan.at[k, i], s5.at[g, k, i], q5.at[g, k, i])
    on5 = {}

    def forward():
        for i in (0, 1, 3, 2):
            for g in range(3):
                fan = bufs["fan"][g]
                for which, k in enumerate((1, 3)):
                    in5[g, k, i].wait_recv()
                    rows = half(g, which)
                    on5[g, which, i] = hop(
                        g,
                        1,
                        k,
                        fan.at[k, i, both, rows],
                        fan.at[2, i, both, rows],
                        s5.at[g, 2 * which, i],
                        q5.at[g, 2 * which, i],
                    )

    out_copies = []
    in6 = []
    for j in (0, 1, 3, 2):
        if j == 1:
            forward()
        for g in range(3):
            ha, hb, hc = here[g]
            fan, sel = bufs["fan"][g], bufs["sel"][g]
            axis_a = GROUP_AXES[g][0]
            if j == 2:
                for i in range(SIDE):
                    on5[g, 0, i].wait_recv()
                    on5[g, 1, i].wait_recv()
            vb = (hb - j + SIDE) % SIDE

            def choose(m, carry, g=g, j=j, ha=ha, hc=hc, vb=vb, axis_a=axis_a, fan=fan, sel=sel):
                vc = (hc - m + SIDE) % SIDE
                dest = number(g, ha, vb, vc)
                for k in range(SIDE):
                    bit = bits[axis_a * SIDE + (ha + k) % SIDE, dest]
                    sel[k, j, vc] = jnp.where(bit > 0, fan[j, m, 1], fan[j, m, 0])
                return carry

            lax.fori_loop(0, SIDE, choose, 0)
            target = home.at[spot(g, ha, vb, every) + (rows_of(g),)]
            for k in (2, 1, 3):
                peer, _ = moved(me, place, axis_a, k)
                copy = send(
                    src_ref=sel.at[k, j],
                    dst_ref=target,
                    send_sem=s6.at[g, k, j],
                    recv_sem=q6.at[g, k, j],
                    device_id=(peer, rep),
                    device_id_type=MESH,
                )
                copy.start()
                in6.append(copy)
                started.append(copy)
            copy = pltpu.make_async_copy(sel.at[0, j], target, out_sem.at[g, j])
            copy.start()
            out_copies.append(copy)

    for copy in out_copies:
        copy.wait()
    for copy in in6:
        copy.wait_recv()
    for copy in started:
        copy.wait_send()


def atom_round(layer_block, sums, w_atom, atoms, bits):
    feat = atoms.shape[1]
    vmem = pl.BlockSpec(memory_space=pltpu.VMEM)
    anywhere = pl.BlockSpec(memory_space=pl.ANY)

    def per_group(*lead):
        return [pltpu.VMEM(lead + (n, 128), BF16) for _, n in GROUP_ROWS]

    dma = pltpu.SemaphoreType.DMA
    scratch = (
        per_group(4, 4, 4)
        + per_group(4, 4, 2)
        + per_group(3, 4, 2)
        + per_group(4, 2)
        + per_group(3, 2)
        + per_group(4, 4, 2)
        + per_group(4, 4, 4)
        + [
            pltpu.VMEM((2, 512, 128), BF16),
            pltpu.VMEM((feat, feat), BF16),
            dma,
            dma((3, 4)),
            dma((3, 4, 4)),
            dma((3, 4, 4)),
            dma((3, 3, 4)),
            dma((3, 3, 4)),
            dma((3, 3)),
            dma((3, 3)),
            dma((3, 4)),
            dma((3, 4)),
            dma((3, 4, 4)),
            dma((3, 4, 4)),
            dma((3, 4, 4)),
            dma((3, 4, 4)),
            dma((3, 4)),
        ]
    )
    home, fresh = pl.pallas_call(
        functools.partial(atoms_kernel, layer_block),
        out_shape=(
            jax.ShapeDtypeStruct((SIDE, SIDE, SIDE, 512, 128), BF16),
            jax.ShapeDtypeStruct(atoms.shape, BF16),
        ),
        in_specs=[pl.BlockSpec(memory_space=pltpu.SMEM), anywhere, anywhere, vmem],
        out_specs=(anywhere, vmem),
        scratch_shapes=scratch,
        name=f"atoms{layer_block}",
        compiler_params=pltpu.CompilerParams(
            collective_id=BLOCKS + layer_block, has_side_effects=True, vmem_limit_bytes=56 << 20
        ),
    )(bits, sums.reshape(SIDE, SIDE, SIDE, 512, 128), w_atom, atoms)
    return home.reshape(PEERS, 512, 128), fresh


def fetch_kernel(owner, first, last, msg, third, keys, home, out, column, blocks, acc, ready, sems):
    count = owner.shape[0]
    step = pl.program_id(0)

    def copy(l):
        return pltpu.make_async_copy(home.at[owner[l]], blocks.at[l], sems.at[l])

    @pl.when(step == 0)
    def _():
        def begin(l, carry):
            copy(l).start()
            return carry

        lax.fori_loop(0, count, begin, 0)
        ready[0] = 0
        to_column(keys, column)

    def finish(l, carry):
        copy(l).wait()
        return carry

    final = step * 4 + 3
    needed = jnp.where(step == 3, count, jnp.minimum(last[final] + 4, count))
    lax.fori_loop(ready[0], needed, finish, 0)
    ready[0] = needed

    for t in range(4):
        tile = step * 4 + t
        rows = pl.ds(t * 128, 128)
        low = first[tile]

        def part(base):
            want = base * ABLK + lax.broadcasted_iota(jnp.int32, (128, 512), 1)
            key = column[pl.ds(pl.multiple_of(tile * 128, 128), 128), :]
            pick = (key == want).astype(F32).astype(BF16)
            at = [jnp.minimum(base + j, count - 1) for j in range(4)]
            block = jnp.concatenate(
                [
                    jnp.concatenate([blocks[at[j], k * 128 : (k + 1) * 128, :] for k in range(4)], axis=1)
                    for j in range(4)
                ],
                axis=0,
            )
            return jnp.dot(pick, block, preferred_element_type=F32)

        base = msg[rows, :].astype(F32) + third[rows, :].astype(F32)
        found = part(low)
        out[rows, :] = (base + found).astype(BF16)

        @pl.when(last[tile] >= low + 4)
        def _():
            acc[...] = msg[rows, :].astype(F32) + third[rows, :].astype(F32) + part(low)

            def more(i, carry):
                acc[...] += part(low + 4 * i)
                return carry

            lax.fori_loop(1, (last[tile] - low) // 4 + 1, more, 0)
            out[rows, :] = acc[...].astype(BF16)


def fetch(message, third, keys, home, owner, first, last):
    rows, feat = message.shape
    lists = owner.shape[0]
    block = pl.BlockSpec((512, feat), lambda i, *_: (i, 0))
    return pl.pallas_call(
        fetch_kernel,
        out_shape=jax.ShapeDtypeStruct((rows, feat), BF16),
        grid_spec=pltpu.PrefetchScalarGridSpec(
            num_scalar_prefetch=3,
            grid=(rows // 512,),
            in_specs=[
                block,
                block,
                pl.BlockSpec((16, 128), lambda i, *_: (0, 0)),
                pl.BlockSpec(memory_space=pl.ANY),
            ],
            out_specs=block,
            scratch_shapes=[
                pltpu.VMEM((rows, 1), jnp.int32),
                pltpu.VMEM((lists, 512, 128), BF16),
                pltpu.VMEM((128, feat), F32),
                pltpu.SMEM((1,), jnp.int32),
                pltpu.SemaphoreType.DMA((lists,)),
            ],
        ),
        name="fetch",
        compiler_params=pltpu.CompilerParams(dimension_semantics=("arbitrary",)),
    )(owner, first, last, message, third, keys, home)


def on_device(
    edge_feats,
    atom_feats,
    w_edge,
    w_atom,
    send_order,
    recv_pos,
    edge_list,
    edge_atom,
    list_block,
    block_home,
):
    lists = list_block.shape[1]
    list_table = jnp.arange(lists, dtype=jnp.int32)
    peer_table = jnp.arange(PEERS, dtype=jnp.int32)
    block_table = jnp.arange(block_home.shape[0], dtype=jnp.int32)
    list_place = jnp.sum(
        jnp.where(list_block[0][:, None] == block_table[None, :], block_home[None, :], 0), axis=1
    )
    owner = list_place // AB_DEV
    placing = owner[None, :] == peer_table[:, None]
    list_of = jnp.max(jnp.where(placing, list_table[None, :], -1), axis=1)
    slot_of = jnp.sum(jnp.where(placing, (list_place % AB_DEV)[None, :], 0), axis=1)
    edge_lists = edge_list[0]
    start = jnp.sum((edge_lists[None, :] < list_table[:, None]).astype(jnp.int32), axis=1)
    tiled_lists = edge_lists.reshape(16, 128)
    first, last = tiled_lists[:, 0], tiled_lists[:, 127]
    keys = edge_lists * ABLK + edge_atom[0]
    keys = keys.reshape(16, 128)
    order = send_order.reshape(-1)
    places = recv_pos.reshape(-1)
    ids = jnp.broadcast_to(jnp.pad(slot_of, (0, 128 - PEERS))[None, :], (8, 128))
    message, atoms = edge_feats, atom_feats
    for layer_block in range(BLOCKS):
        pair, all_ids = exchange(layer_block, message, w_edge, order, places, ids)
        if layer_block == 0:
            bits = all_ids[:, 0, :]
        third, sums = list_sums(layer_block, pair, w_edge, keys, list_of, owner, start)
        home, atoms = atom_round(layer_block, sums, w_atom, atoms, bits)
        message = fetch(message, third, keys, home, owner, first, last)
    return message, atoms


def solution(mesh):
    split = P(("rep", "edge"), None)
    whole = P(None, None, None)
    return jax.shard_map(
        on_device,
        mesh=mesh,
        in_specs=(split, split, whole, whole, split, split, split, split, split, P("rep")),
        out_specs=(split, split),
        check_vma=False,
    )
```

```python
import functools

import jax
import jax.numpy as jnp
from jax import lax
from jax.experimental import pallas as pl
from jax.experimental.pallas import tpu as pltpu
from jax.sharding import PartitionSpec as P

ABLK = 128
BLOCKS = 2
AB_DEV = 2
SIDE = 4
PEERS = SIDE * SIDE * SIDE
STRIDES = (16, 4, 1)
GROUP_AXES = ((0, 1, 2), (1, 2, 0), (2, 0, 1))
GROUP_ROWS = ((0, 176), (176, 176), (352, 160))
MESH = pl.DeviceIdType.MESH
F32 = jnp.float32
BF16 = jnp.bfloat16
STAGGER = 26000
DENSE_ROWS = 512


def silu(v):
    half = 0.5 * v
    return half + half * jnp.tanh(half)


def to_column(rows, column):
    turned = jnp.transpose(rows[...])
    for t in range(16):
        column[t * 128 : (t + 1) * 128, :] = turned[:, t : t + 1]


def coords(me):
    return [(me // s) % SIDE for s in STRIDES]


def moved(me, place, axis, step):
    new = (place[axis] + step) % SIDE
    return me + (new - place[axis]) * STRIDES[axis], new


def peer_at(me, i, sign):
    i0, i1, i2 = i % 4, (i // 4) % 4, i // 16
    dx, dz, dy = i0, i1 + i0, i2 + i1 + i0
    px = (me // 16 + sign * dx + 16) % 4
    pz = ((me // 4) % 4 + sign * dz + 16) % 4
    py = (me % 4 + sign * dy + 16) % 4
    return px * 16 + pz * 4 + py


def exchange_kernel(
    layer_block,
    msg,
    w_hbm,
    order,
    places,
    ids,
    paired,
    ids_out,
    weights,
    tall,
    outgoing,
    arrived,
    w_sem,
    send_sem,
    recv_sem,
    id_send,
    id_recv,
):
    me = lax.axis_index("edge")
    rep = lax.axis_index("rep")
    place = coords(me)
    barrier = pltpu.get_barrier_semaphore()
    load = pltpu.make_async_copy(w_hbm.at[pl.ds(3 * layer_block, 2)], weights, w_sem)
    load.start()

    def greet(i, carry):
        peer = me + i
        peer = jnp.where(peer >= PEERS, peer - PEERS, peer)
        pl.semaphore_signal(barrier, inc=1, device_id=(peer, rep), device_id_type=MESH)
        return carry

    lax.fori_loop(1, PEERS, greet, 0)
    if layer_block == 0:

        @pl.when(rep == 1)
        def _():
            pl.delay(STAGGER)

    load.wait()

    def dense(c, carry):
        rows = pl.ds(pl.multiple_of(c * DENSE_ROWS, DENSE_ROWS), DENSE_ROWS)
        first = silu(jnp.dot(msg[rows, :], weights[0], preferred_element_type=F32)).astype(BF16)
        value = silu(jnp.dot(first, weights[1], preferred_element_type=F32)).astype(BF16).astype(F32)
        tall[rows] = value.reshape(DENSE_ROWS, 4, 128)
        return carry

    lax.fori_loop(0, msg.shape[0] // DENSE_ROWS, dense, 0)
    pl.semaphore_wait(barrier, PEERS - 1)

    id_copies = []
    for axis in range(3):
        ids_out[pl.ds(axis * SIDE + place[axis], 1)] = ids[...][None]
        for step in range(1, SIDE):
            peer, _ = moved(me, place, axis, step)
            copy = pltpu.make_async_remote_copy(
                src_ref=ids,
                dst_ref=ids_out.at[axis * SIDE + place[axis]],
                send_sem=id_send.at[axis * 3 + step - 1],
                recv_sem=id_recv.at[axis * 3 + step - 1],
                device_id=(peer, rep),
                device_id_type=MESH,
            )
            copy.start()
            id_copies.append(copy)

    def message(i, source):
        return pltpu.make_async_remote_copy(
            src_ref=outgoing.at[pl.ds(i * 32, 32)],
            dst_ref=arrived.at[pl.ds(source * 32, 32)],
            send_sem=send_sem.at[i],
            recv_sem=recv_sem.at[i],
            device_id=(peer_at(me, i, 1), rep),
            device_id_type=MESH,
        )

    def row_of(t):
        return tall[order[t]].astype(BF16)

    for k in range(32):
        arrived[me * 32 + k] = row_of(me * 32 + k)

    def send_one(i, carry):
        peer = peer_at(me, i, 1)
        for k in range(32):
            outgoing[i * 32 + k] = row_of(peer * 32 + k)
        message(i, me).start()
        return carry

    lax.fori_loop(1, PEERS, send_one, 0)

    def arrive(i, carry):
        message(i, peer_at(me, i, -1)).wait_recv()
        return carry

    lax.fori_loop(1, PEERS, arrive, 0)

    def add(c, carry):
        for k in range(32):
            row = c * 32 + k
            tall[row] = tall[row] + arrived[places[row]].astype(F32)
        rows = pl.ds(pl.multiple_of(c * 32, 32), 32)
        paired[rows, :] = tall[rows].reshape(32, 4 * 128).astype(BF16)
        return carry

    lax.fori_loop(0, PEERS, add, 0)

    def finish(i, carry):
        message(i, me).wait_send()
        return carry

    lax.fori_loop(1, PEERS, finish, 0)
    for copy in id_copies:
        copy.wait()


def exchange(layer_block, message, w_edge, order, places, ids):
    rows, feat = message.shape
    vmem = pl.BlockSpec(memory_space=pltpu.VMEM)
    smem = pl.BlockSpec(memory_space=pltpu.SMEM)
    return pl.pallas_call(
        functools.partial(exchange_kernel, layer_block),
        out_shape=(
            jax.ShapeDtypeStruct((rows, feat), BF16),
            jax.ShapeDtypeStruct((3 * SIDE, 8, 128), jnp.int32),
        ),
        in_specs=[vmem, pl.BlockSpec(memory_space=pl.ANY), smem, smem, vmem],
        out_specs=(vmem, vmem),
        scratch_shapes=[
            pltpu.VMEM((2, feat, feat), BF16),
            pltpu.VMEM((rows, 4, 128), F32),
            pltpu.VMEM((rows, 4, 128), BF16),
            pltpu.VMEM((rows, 4, 128), BF16),
            pltpu.SemaphoreType.DMA,
            pltpu.SemaphoreType.DMA((PEERS,)),
            pltpu.SemaphoreType.DMA((PEERS,)),
            pltpu.SemaphoreType.DMA((9,)),
            pltpu.SemaphoreType.DMA((9,)),
        ],
        name=f"exchange{layer_block}",
        compiler_params=pltpu.CompilerParams(collective_id=layer_block, has_side_effects=True),
    )(message, w_edge, order, places, ids)


def sums_kernel(layer_block, list_of, owner, start, pair, w_hbm, keys, third, out, weight, sums, zero, w_sem, sems):
    load = pltpu.make_async_copy(w_hbm.at[3 * layer_block + 2], weight, w_sem)
    load.start()
    zero[...] = jnp.zeros(zero.shape, BF16)

    def clear(d, carry):
        @pl.when(list_of[d] < 0)
        def _():
            pltpu.make_async_copy(zero, out.at[d], sems.at[d]).start()

        return carry

    lax.fori_loop(0, PEERS, clear, 0)
    load.wait()

    def dense(c, carry):
        rows = pl.ds(pl.multiple_of(c * 512, 512), 512)
        value = silu(jnp.dot(pair[rows, :], weight[...], preferred_element_type=F32))
        third[rows, :] = value.astype(BF16)
        return carry

    lax.fori_loop(0, 4, dense, 0)

    def one(l, carry):
        begin = jnp.minimum(start[l] // 128, 13)
        key = jnp.concatenate([keys[pl.ds(begin + t, 1), :] for t in range(3)], axis=1)
        want = l * ABLK + lax.broadcasted_iota(jnp.int32, (ABLK, 384), 0)
        pick = (key == want).astype(F32).astype(BF16)
        rows = third[pl.ds(pl.multiple_of(begin * 128, 128), 384), :]
        value = jnp.dot(pick, rows, preferred_element_type=F32).astype(BF16)
        for k in range(4):
            sums[l, k * 128 : (k + 1) * 128, :] = value[:, k * 128 : (k + 1) * 128]
        pltpu.make_async_copy(sums.at[l], out.at[owner[l]], sems.at[owner[l]]).start()
        return carry

    lax.fori_loop(0, owner.shape[0], one, 0, unroll=4)

    def finish(d, carry):
        pltpu.make_async_copy(zero, out.at[d], sems.at[d]).wait()
        return carry

    lax.fori_loop(0, PEERS, finish, 0)


def list_sums(layer_block, pair, w_edge, keys, list_of, owner, start):
    rows, feat = pair.shape
    vmem = pl.BlockSpec(memory_space=pltpu.VMEM)
    smem = pl.BlockSpec(memory_space=pltpu.SMEM)
    anywhere = pl.BlockSpec(memory_space=pl.ANY)
    return pl.pallas_call(
        functools.partial(sums_kernel, layer_block),
        out_shape=(
            jax.ShapeDtypeStruct((rows, feat), BF16),
            jax.ShapeDtypeStruct((PEERS, 512, 128), BF16),
        ),
        in_specs=[smem, smem, smem, vmem, anywhere, vmem],
        out_specs=(vmem, anywhere),
        scratch_shapes=[
            pltpu.VMEM((feat, feat), BF16),
            pltpu.VMEM((owner.shape[0], 512, 128), BF16),
            pltpu.VMEM((512, 128), BF16),
            pltpu.SemaphoreType.DMA,
            pltpu.SemaphoreType.DMA((PEERS,)),
        ],
        name=f"sums{layer_block}",
    )(list_of, owner, start, pair, w_edge, keys)


def atoms_kernel(layer_block, bits, sums, w_hbm, atoms, home, atoms_out, *scratch):
    names = ["r1", "t1", "r2", "t2", "r3", "fan", "sel"]
    bufs = {name: scratch[3 * n : 3 * n + 3] for n, name in enumerate(names)}
    flat, weight, w_sem, own_sem, s1, q1, s2, q2, s3, q3, s4, q4, s5, q5, s6, q6, out_sem = scratch[21:]
    me = lax.axis_index("edge")
    rep = lax.axis_index("rep")
    place = coords(me)
    barrier = pltpu.get_barrier_semaphore()
    for axis in range(3):
        for step in range(1, SIDE):
            peer, _ = moved(me, place, axis, step)
            pl.semaphore_signal(barrier, inc=1, device_id=(peer, rep), device_id_type=MESH)
    load = pltpu.make_async_copy(w_hbm.at[layer_block], weight, w_sem)
    load.start()

    def spot(g, va, vb, vc):
        index = [None] * 3
        for axis, value in zip(GROUP_AXES[g], (va, vb, vc)):
            index[axis] = value
        return tuple(index)

    def number(g, va, vb, vc):
        x, z, y = spot(g, va, vb, vc)
        return x * 16 + z * 4 + y

    def rows_of(g):
        return pl.ds(GROUP_ROWS[g][0], GROUP_ROWS[g][1])

    every = pl.ds(0, SIDE)
    send = pltpu.make_async_remote_copy
    here = [[place[axis] for axis in GROUP_AXES[g]] for g in range(3)]
    started = []

    own_copies = {}
    for j in range(SIDE):
        for g in range(3):
            ha, hb, hc = here[g]
            vb = (hb + 1 + j) % SIDE
            copy = pltpu.make_async_copy(
                sums.at[spot(g, ha, vb, every) + (rows_of(g),)], bufs["r1"][g].at[0, j], own_sem.at[g, j]
            )
            copy.start()
            own_copies[g, j] = copy
    pl.semaphore_wait(barrier, 9)

    in1 = {}
    for j in range(SIDE):
        for k in (2, 1, 3):
            for g in range(3):
                ha, hb, hc = here[g]
                peer, va = moved(me, place, GROUP_AXES[g][0], k)
                vb = (hb + 1 + j) % SIDE
                copy = send(
                    src_ref=sums.at[spot(g, va, vb, every) + (rows_of(g),)],
                    dst_ref=bufs["r1"][g].at[k, j],
                    send_sem=s1.at[g, k, j],
                    recv_sem=q1.at[g, k, j],
                    device_id=(peer, rep),
                    device_id_type=MESH,
                )
                copy.start()
                in1[g, k, j] = copy
                started.append(copy)

    in2 = {}
    for j in range(SIDE):
        for g in range(3):
            ha, hb, hc = here[g]
            n = GROUP_ROWS[g][1]
            axis_a = GROUP_AXES[g][0]
            vb = (hb + 1 + j) % SIDE
            own_copies[g, j].wait()
            for k in range(1, SIDE):
                in1[g, k, j].wait_recv()
            r1, t1 = bufs["r1"][g], bufs["t1"][g]

            def one(m, carry, g=g, j=j, ha=ha, hb=hb, hc=hc, vb=vb, axis_a=axis_a, r1=r1, t1=t1, n=n):
                dest = number(g, ha, vb, m)
                low = jnp.zeros((n, 128), F32)
                high = jnp.zeros((n, 128), F32)
                for k in range(SIDE):
                    source = (ha - k + SIDE) % SIDE
                    bit = bits[axis_a * SIDE + source, dest].astype(F32)
                    value = r1[k, j, m].astype(F32)
                    upper = value * bit
                    high = high + upper
                    low = low + (value - upper)
                t1[j, m, 0] = low.astype(BF16)
                t1[j, m, 1] = high.astype(BF16)
                return carry

            lax.fori_loop(0, SIDE, one, 0)
            if j < SIDE - 1:
                peer, _ = moved(me, place, GROUP_AXES[g][1], 1 + j)
                for i in range(SIDE):
                    vc = (hc + 1 + i) % SIDE
                    copy = send(
                        src_ref=t1.at[j, vc],
                        dst_ref=bufs["r2"][g].at[j, vc],
                        send_sem=s2.at[g, j, i],
                        recv_sem=q2.at[g, j, i],
                        device_id=(peer, rep),
                        device_id_type=MESH,
                    )
                    copy.start()
                    in2[g, j, i] = copy
                    started.append(copy)

    in3 = {}
    for i in range(SIDE):
        for g in range(3):
            ha, hb, hc = here[g]
            vc = (hc + 1 + i) % SIDE
            for j in range(SIDE - 1):
                in2[g, j, i].wait_recv()
            t1, r2, t2 = bufs["t1"][g], bufs["r2"][g], bufs["t2"][g]
            for slot in range(AB_DEV):
                value = t1[SIDE - 1, vc, slot].astype(F32)
                for j in range(SIDE - 1):
                    value = value + r2[j, vc, slot].astype(F32)
                t2[i, slot] = value.astype(BF16)
            if i < SIDE - 1:
                peer, _ = moved(me, place, GROUP_AXES[g][2], 1 + i)
                copy = send(
                    src_ref=t2.at[i],
                    dst_ref=bufs["r3"][g].at[i],
                    send_sem=s3.at[g, i],
                    recv_sem=q3.at[g, i],
                    device_id=(peer, rep),
                    device_id_type=MESH,
                )
                copy.start()
                in3[g, i] = copy
                started.append(copy)

    for g in range(3):
        for i in range(SIDE - 1):
            in3[g, i].wait_recv()
        t2, r3 = bufs["t2"][g], bufs["r3"][g]
        for slot in range(AB_DEV):
            value = t2[SIDE - 1, slot].astype(F32)
            for i in range(SIDE - 1):
                value = value + r3[i, slot].astype(F32)
            flat[slot, rows_of(g), :] = value.astype(BF16)

    load.wait()
    for slot in range(AB_DEV):
        gathered = jnp.concatenate([flat[slot, k * 128 : (k + 1) * 128, :] for k in range(4)], axis=1)
        update = silu(jnp.dot(gathered, weight[...], preferred_element_type=F32))
        rows = slice(slot * ABLK, (slot + 1) * ABLK)
        fresh = (atoms[rows, :].astype(F32) + update).astype(BF16)
        atoms_out[rows, :] = fresh
        for k in range(4):
            flat[slot, k * 128 : (k + 1) * 128, :] = fresh[:, k * 128 : (k + 1) * 128]
    in4 = {}

    def hop(g, axis_at, step, source, target, send_sem, recv_sem):
        peer, _ = moved(me, place, GROUP_AXES[g][axis_at], step)
        copy = send(
            src_ref=source,
            dst_ref=target,
            send_sem=send_sem,
            recv_sem=recv_sem,
            device_id=(peer, rep),
            device_id_type=MESH,
        )
        copy.start()
        started.append(copy)
        return copy

    def half(g, which):
        n = GROUP_ROWS[g][1]
        cut = (n // 32) * 16 + (n // 16) % 2 * 16
        return pl.ds(0, cut) if which == 0 else pl.ds(cut, n - cut)

    both = pl.ds(0, AB_DEV)
    for g in range(3):
        fan = bufs["fan"][g]
        fan[0, 0] = flat[:, rows_of(g), :]
        for k in (1, 3):
            in4[g, k] = hop(g, 2, k, fan.at[0, 0], fan.at[0, k], s4.at[g, k], q4.at[g, k])
    on4 = {}
    for g in range(3):
        fan = bufs["fan"][g]
        for which, k in enumerate((1, 3)):
            in4[g, k].wait_recv()
            rows = half(g, which)
            on4[g, which] = hop(
                g,
                2,
                k,
                fan.at[0, k, both, rows],
                fan.at[0, 2, both, rows],
                s4.at[g, 2 * which],
                q4.at[g, 2 * which],
            )

    in5 = {}
    for i in (0, 1, 3, 2):
        for g in range(3):
            fan = bufs["fan"][g]
            if i == 2:
                on4[g, 0].wait_recv()
                on4[g, 1].wait_recv()
            for k in (1, 3):
                in5[g, k, i] = hop(g, 1, k, fan.at[0, i], fan.at[k, i], s5.at[g, k, i], q5.at[g, k, i])
    on5 = {}

    def forward():
        for i in (0, 1, 3, 2):
            for g in range(3):
                fan = bufs["fan"][g]
                for which, k in enumerate((1, 3)):
                    in5[g, k, i].wait_recv()
                    rows = half(g, which)
                    on5[g, which, i] = hop(
                        g,
                        1,
                        k,
                        fan.at[k, i, both, rows],
                        fan.at[2, i, both, rows],
                        s5.at[g, 2 * which, i],
                        q5.at[g, 2 * which, i],
                    )

    out_copies = []
    in6 = []
    for j in (0, 1, 3, 2):
        if j == 1:
            forward()
        for g in range(3):
            ha, hb, hc = here[g]
            fan, sel = bufs["fan"][g], bufs["sel"][g]
            axis_a = GROUP_AXES[g][0]
            if j == 2:
                for i in range(SIDE):
                    on5[g, 0, i].wait_recv()
                    on5[g, 1, i].wait_recv()
            vb = (hb - j + SIDE) % SIDE

            def choose(m, carry, g=g, j=j, ha=ha, hc=hc, vb=vb, axis_a=axis_a, fan=fan, sel=sel):
                vc = (hc - m + SIDE) % SIDE
                dest = number(g, ha, vb, vc)
                for k in range(SIDE):
                    bit = bits[axis_a * SIDE + (ha + k) % SIDE, dest]
                    sel[k, j, vc] = jnp.where(bit > 0, fan[j, m, 1], fan[j, m, 0])
                return carry

            lax.fori_loop(0, SIDE, choose, 0)
            target = home.at[spot(g, ha, vb, every) + (rows_of(g),)]
            for k in (2, 1, 3):
                peer, _ = moved(me, place, axis_a, k)
                copy = send(
                    src_ref=sel.at[k, j],
                    dst_ref=target,
                    send_sem=s6.at[g, k, j],
                    recv_sem=q6.at[g, k, j],
                    device_id=(peer, rep),
                    device_id_type=MESH,
                )
                copy.start()
                in6.append(copy)
                started.append(copy)
            copy = pltpu.make_async_copy(sel.at[0, j], target, out_sem.at[g, j])
            copy.start()
            out_copies.append(copy)

    for copy in out_copies:
        copy.wait()
    for copy in in6:
        copy.wait_recv()
    for copy in started:
        copy.wait_send()


def atom_round(layer_block, sums, w_atom, atoms, bits):
    feat = atoms.shape[1]
    vmem = pl.BlockSpec(memory_space=pltpu.VMEM)
    anywhere = pl.BlockSpec(memory_space=pl.ANY)

    def per_group(*lead):
        return [pltpu.VMEM(lead + (n, 128), BF16) for _, n in GROUP_ROWS]

    dma = pltpu.SemaphoreType.DMA
    scratch = (
        per_group(4, 4, 4)
        + per_group(4, 4, 2)
        + per_group(3, 4, 2)
        + per_group(4, 2)
        + per_group(3, 2)
        + per_group(4, 4, 2)
        + per_group(4, 4, 4)
        + [
            pltpu.VMEM((2, 512, 128), BF16),
            pltpu.VMEM((feat, feat), BF16),
            dma,
            dma((3, 4)),
            dma((3, 4, 4)),
            dma((3, 4, 4)),
            dma((3, 3, 4)),
            dma((3, 3, 4)),
            dma((3, 3)),
            dma((3, 3)),
            dma((3, 4)),
            dma((3, 4)),
            dma((3, 4, 4)),
            dma((3, 4, 4)),
            dma((3, 4, 4)),
            dma((3, 4, 4)),
            dma((3, 4)),
        ]
    )
    home, fresh = pl.pallas_call(
        functools.partial(atoms_kernel, layer_block),
        out_shape=(
            jax.ShapeDtypeStruct((SIDE, SIDE, SIDE, 512, 128), BF16),
            jax.ShapeDtypeStruct(atoms.shape, BF16),
        ),
        in_specs=[pl.BlockSpec(memory_space=pltpu.SMEM), anywhere, anywhere, vmem],
        out_specs=(anywhere, vmem),
        scratch_shapes=scratch,
        name=f"atoms{layer_block}",
        compiler_params=pltpu.CompilerParams(
            collective_id=BLOCKS + layer_block, has_side_effects=True, vmem_limit_bytes=56 << 20
        ),
    )(bits, sums.reshape(SIDE, SIDE, SIDE, 512, 128), w_atom, atoms)
    return home.reshape(PEERS, 512, 128), fresh


def fetch_kernel(owner, first, last, msg, third, keys, home, out, column, blocks, acc, ready, sems):
    count = owner.shape[0]
    step = pl.program_id(0)

    def copy(l):
        return pltpu.make_async_copy(home.at[owner[l]], blocks.at[l], sems.at[l])

    @pl.when(step == 0)
    def _():
        def begin(l, carry):
            copy(l).start()
            return carry

        lax.fori_loop(0, count, begin, 0)
        ready[0] = 0
        to_column(keys, column)

    def finish(l, carry):
        copy(l).wait()
        return carry

    final = step * 4 + 3
    needed = jnp.where(step == 3, count, jnp.minimum(last[final] + 4, count))
    lax.fori_loop(ready[0], needed, finish, 0)
    ready[0] = needed

    for t in range(4):
        tile = step * 4 + t
        rows = pl.ds(t * 128, 128)
        low = first[tile]

        def part(base):
            want = base * ABLK + lax.broadcasted_iota(jnp.int32, (128, 512), 1)
            key = column[pl.ds(pl.multiple_of(tile * 128, 128), 128), :]
            pick = (key == want).astype(F32).astype(BF16)
            at = [jnp.minimum(base + j, count - 1) for j in range(4)]
            block = jnp.concatenate(
                [
                    jnp.concatenate([blocks[at[j], k * 128 : (k + 1) * 128, :] for k in range(4)], axis=1)
                    for j in range(4)
                ],
                axis=0,
            )
            return jnp.dot(pick, block, preferred_element_type=F32)

        base = msg[rows, :].astype(F32) + third[rows, :].astype(F32)
        found = part(low)
        out[rows, :] = (base + found).astype(BF16)

        @pl.when(last[tile] >= low + 4)
        def _():
            acc[...] = msg[rows, :].astype(F32) + third[rows, :].astype(F32) + part(low)

            def more(i, carry):
                acc[...] += part(low + 4 * i)
                return carry

            lax.fori_loop(1, (last[tile] - low) // 4 + 1, more, 0)
            out[rows, :] = acc[...].astype(BF16)


def fetch(message, third, keys, home, owner, first, last):
    rows, feat = message.shape
    lists = owner.shape[0]
    block = pl.BlockSpec((512, feat), lambda i, *_: (i, 0))
    return pl.pallas_call(
        fetch_kernel,
        out_shape=jax.ShapeDtypeStruct((rows, feat), BF16),
        grid_spec=pltpu.PrefetchScalarGridSpec(
            num_scalar_prefetch=3,
            grid=(rows // 512,),
            in_specs=[
                block,
                block,
                pl.BlockSpec((16, 128), lambda i, *_: (0, 0)),
                pl.BlockSpec(memory_space=pl.ANY),
            ],
            out_specs=block,
            scratch_shapes=[
                pltpu.VMEM((rows, 1), jnp.int32),
                pltpu.VMEM((lists, 512, 128), BF16),
                pltpu.VMEM((128, feat), F32),
                pltpu.SMEM((1,), jnp.int32),
                pltpu.SemaphoreType.DMA((lists,)),
            ],
        ),
        name="fetch",
        compiler_params=pltpu.CompilerParams(dimension_semantics=("arbitrary",)),
    )(owner, first, last, message, third, keys, home)


def on_device(
    edge_feats,
    atom_feats,
    w_edge,
    w_atom,
    send_order,
    recv_pos,
    edge_list,
    edge_atom,
    list_block,
    block_home,
):
    lists = list_block.shape[1]
    list_table = jnp.arange(lists, dtype=jnp.int32)
    peer_table = jnp.arange(PEERS, dtype=jnp.int32)
    block_table = jnp.arange(block_home.shape[0], dtype=jnp.int32)
    list_place = jnp.sum(
        jnp.where(list_block[0][:, None] == block_table[None, :], block_home[None, :], 0), axis=1
    )
    owner = list_place // AB_DEV
    placing = owner[None, :] == peer_table[:, None]
    list_of = jnp.max(jnp.where(placing, list_table[None, :], -1), axis=1)
    slot_of = jnp.sum(jnp.where(placing, (list_place % AB_DEV)[None, :], 0), axis=1)
    edge_lists = edge_list[0]
    start = jnp.sum((edge_lists[None, :] < list_table[:, None]).astype(jnp.int32), axis=1)
    tiled_lists = edge_lists.reshape(16, 128)
    first, last = tiled_lists[:, 0], tiled_lists[:, 127]
    keys = edge_lists * ABLK + edge_atom[0]
    keys = keys.reshape(16, 128)
    order = send_order.reshape(-1)
    places = recv_pos.reshape(-1)
    ids = jnp.broadcast_to(jnp.pad(slot_of, (0, 128 - PEERS))[None, :], (8, 128))
    message, atoms = edge_feats, atom_feats
    for layer_block in range(BLOCKS):
        pair, all_ids = exchange(layer_block, message, w_edge, order, places, ids)
        if layer_block == 0:
            bits = all_ids[:, 0, :]
        third, sums = list_sums(layer_block, pair, w_edge, keys, list_of, owner, start)
        home, atoms = atom_round(layer_block, sums, w_atom, atoms, bits)
        message = fetch(message, third, keys, home, owner, first, last)
    return message, atoms


def solution(mesh):
    split = P(("rep", "edge"), None)
    whole = P(None, None, None)
    return jax.shard_map(
        on_device,
        mesh=mesh,
        in_specs=(split, split, whole, whole, split, split, split, split, split, P("rep")),
        out_specs=(split, split),
        check_vma=False,
    )
```

```python
import functools

import jax
import jax.numpy as jnp
from jax import lax
from jax.experimental import pallas as pl
from jax.experimental.pallas import tpu as pltpu
from jax.sharding import PartitionSpec as P

ABLK = 128
BLOCKS = 2
AB_DEV = 2
SIDE = 4
PEERS = SIDE * SIDE * SIDE
STRIDES = (16, 4, 1)
GROUP_AXES = ((0, 1, 2), (1, 2, 0), (2, 0, 1))
GROUP_ROWS = ((0, 176), (176, 176), (352, 160))
MESH = pl.DeviceIdType.MESH
F32 = jnp.float32
BF16 = jnp.bfloat16
STAGGER = 25000
DENSE_ROWS = 512


def silu(v):
    half = 0.5 * v
    return half + half * jnp.tanh(half)


def to_column(rows, column):
    turned = jnp.transpose(rows[...])
    for t in range(16):
        column[t * 128 : (t + 1) * 128, :] = turned[:, t : t + 1]


def coords(me):
    return [(me // s) % SIDE for s in STRIDES]


def moved(me, place, axis, step):
    new = (place[axis] + step) % SIDE
    return me + (new - place[axis]) * STRIDES[axis], new


def peer_at(me, i, sign):
    i0, i1, i2 = i % 4, (i // 4) % 4, i // 16
    dx, dz, dy = i0, i1 + i0, i2 + i1 + i0
    px = (me // 16 + sign * dx + 16) % 4
    pz = ((me // 4) % 4 + sign * dz + 16) % 4
    py = (me % 4 + sign * dy + 16) % 4
    return px * 16 + pz * 4 + py


def exchange_kernel(
    layer_block,
    msg,
    w_hbm,
    order,
    places,
    ids,
    paired,
    ids_out,
    weights,
    tall,
    outgoing,
    arrived,
    w_sem,
    send_sem,
    recv_sem,
    id_send,
    id_recv,
):
    me = lax.axis_index("edge")
    rep = lax.axis_index("rep")
    place = coords(me)
    barrier = pltpu.get_barrier_semaphore()
    load = pltpu.make_async_copy(w_hbm.at[pl.ds(3 * layer_block, 2)], weights, w_sem)
    load.start()

    def greet(i, carry):
        peer = me + i
        peer = jnp.where(peer >= PEERS, peer - PEERS, peer)
        pl.semaphore_signal(barrier, inc=1, device_id=(peer, rep), device_id_type=MESH)
        return carry

    lax.fori_loop(1, PEERS, greet, 0)
    if layer_block == 0:

        @pl.when(rep == 1)
        def _():
            pl.delay(STAGGER)

    load.wait()

    def dense(c, carry):
        rows = pl.ds(pl.multiple_of(c * DENSE_ROWS, DENSE_ROWS), DENSE_ROWS)
        first = silu(jnp.dot(msg[rows, :], weights[0], preferred_element_type=F32)).astype(BF16)
        value = silu(jnp.dot(first, weights[1], preferred_element_type=F32)).astype(BF16).astype(F32)
        tall[rows] = value.reshape(DENSE_ROWS, 4, 128)
        return carry

    lax.fori_loop(0, msg.shape[0] // DENSE_ROWS, dense, 0)
    pl.semaphore_wait(barrier, PEERS - 1)

    id_copies = []
    for axis in range(3):
        ids_out[pl.ds(axis * SIDE + place[axis], 1)] = ids[...][None]
        for step in range(1, SIDE):
            peer, _ = moved(me, place, axis, step)
            copy = pltpu.make_async_remote_copy(
                src_ref=ids,
                dst_ref=ids_out.at[axis * SIDE + place[axis]],
                send_sem=id_send.at[axis * 3 + step - 1],
                recv_sem=id_recv.at[axis * 3 + step - 1],
                device_id=(peer, rep),
                device_id_type=MESH,
            )
            copy.start()
            id_copies.append(copy)

    def message(i, source):
        return pltpu.make_async_remote_copy(
            src_ref=outgoing.at[pl.ds(i * 32, 32)],
            dst_ref=arrived.at[pl.ds(source * 32, 32)],
            send_sem=send_sem.at[i],
            recv_sem=recv_sem.at[i],
            device_id=(peer_at(me, i, 1), rep),
            device_id_type=MESH,
        )

    def row_of(t):
        return tall[order[t]].astype(BF16)

    for k in range(32):
        arrived[me * 32 + k] = row_of(me * 32 + k)

    def send_one(i, carry):
        peer = peer_at(me, i, 1)
        for k in range(32):
            outgoing[i * 32 + k] = row_of(peer * 32 + k)
        message(i, me).start()
        return carry

    lax.fori_loop(1, PEERS, send_one, 0)

    def arrive(i, carry):
        message(i, peer_at(me, i, -1)).wait_recv()
        return carry

    lax.fori_loop(1, PEERS, arrive, 0)

    def add(c, carry):
        for k in range(32):
            row = c * 32 + k
            tall[row] = tall[row] + arrived[places[row]].astype(F32)
        rows = pl.ds(pl.multiple_of(c * 32, 32), 32)
        paired[rows, :] = tall[rows].reshape(32, 4 * 128).astype(BF16)
        return carry

    lax.fori_loop(0, PEERS, add, 0, unroll=2)

    def finish(i, carry):
        message(i, me).wait_send()
        return carry

    lax.fori_loop(1, PEERS, finish, 0)
    for copy in id_copies:
        copy.wait()


def exchange(layer_block, message, w_edge, order, places, ids):
    rows, feat = message.shape
    vmem = pl.BlockSpec(memory_space=pltpu.VMEM)
    smem = pl.BlockSpec(memory_space=pltpu.SMEM)
    return pl.pallas_call(
        functools.partial(exchange_kernel, layer_block),
        out_shape=(
            jax.ShapeDtypeStruct((rows, feat), BF16),
            jax.ShapeDtypeStruct((3 * SIDE, 8, 128), jnp.int32),
        ),
        in_specs=[vmem, pl.BlockSpec(memory_space=pl.ANY), smem, smem, vmem],
        out_specs=(vmem, vmem),
        scratch_shapes=[
            pltpu.VMEM((2, feat, feat), BF16),
            pltpu.VMEM((rows, 4, 128), F32),
            pltpu.VMEM((rows, 4, 128), BF16),
            pltpu.VMEM((rows, 4, 128), BF16),
            pltpu.SemaphoreType.DMA,
            pltpu.SemaphoreType.DMA((PEERS,)),
            pltpu.SemaphoreType.DMA((PEERS,)),
            pltpu.SemaphoreType.DMA((9,)),
            pltpu.SemaphoreType.DMA((9,)),
        ],
        name=f"exchange{layer_block}",
        compiler_params=pltpu.CompilerParams(collective_id=layer_block, has_side_effects=True),
    )(message, w_edge, order, places, ids)


def sums_kernel(layer_block, list_of, owner, start, pair, w_hbm, keys, third, out, weight, sums, zero, w_sem, sems):
    load = pltpu.make_async_copy(w_hbm.at[3 * layer_block + 2], weight, w_sem)
    load.start()
    zero[...] = jnp.zeros(zero.shape, BF16)

    def clear(d, carry):
        @pl.when(list_of[d] < 0)
        def _():
            pltpu.make_async_copy(zero, out.at[d], sems.at[d]).start()

        return carry

    lax.fori_loop(0, PEERS, clear, 0)
    load.wait()

    def dense(c, carry):
        rows = pl.ds(pl.multiple_of(c * 1024, 1024), 1024)
        value = silu(jnp.dot(pair[rows, :], weight[...], preferred_element_type=F32))
        third[rows, :] = value.astype(BF16)
        return carry

    lax.fori_loop(0, 2, dense, 0)

    def one(l, carry):
        begin = jnp.minimum(start[l] // 128, 13)
        key = jnp.concatenate([keys[pl.ds(begin + t, 1), :] for t in range(3)], axis=1)
        want = l * ABLK + lax.broadcasted_iota(jnp.int32, (ABLK, 384), 0)
        pick = (key == want).astype(F32).astype(BF16)
        rows = third[pl.ds(pl.multiple_of(begin * 128, 128), 384), :]
        value = jnp.dot(pick, rows, preferred_element_type=F32).astype(BF16)
        for k in range(4):
            sums[l, k * 128 : (k + 1) * 128, :] = value[:, k * 128 : (k + 1) * 128]
        pltpu.make_async_copy(sums.at[l], out.at[owner[l]], sems.at[owner[l]]).start()
        return carry

    lax.fori_loop(0, owner.shape[0], one, 0, unroll=8)

    def finish(d, carry):
        pltpu.make_async_copy(zero, out.at[d], sems.at[d]).wait()
        return carry

    lax.fori_loop(0, PEERS, finish, 0)


def list_sums(layer_block, pair, w_edge, keys, list_of, owner, start):
    rows, feat = pair.shape
    vmem = pl.BlockSpec(memory_space=pltpu.VMEM)
    smem = pl.BlockSpec(memory_space=pltpu.SMEM)
    anywhere = pl.BlockSpec(memory_space=pl.ANY)
    return pl.pallas_call(
        functools.partial(sums_kernel, layer_block),
        out_shape=(
            jax.ShapeDtypeStruct((rows, feat), BF16),
            jax.ShapeDtypeStruct((PEERS, 512, 128), BF16),
        ),
        in_specs=[smem, smem, smem, vmem, anywhere, vmem],
        out_specs=(vmem, anywhere),
        scratch_shapes=[
            pltpu.VMEM((feat, feat), BF16),
            pltpu.VMEM((owner.shape[0], 512, 128), BF16),
            pltpu.VMEM((512, 128), BF16),
            pltpu.SemaphoreType.DMA,
            pltpu.SemaphoreType.DMA((PEERS,)),
        ],
        name=f"sums{layer_block}",
    )(list_of, owner, start, pair, w_edge, keys)


def atoms_kernel(layer_block, bits, sums, w_hbm, atoms, home, atoms_out, *scratch):
    names = ["r1", "t1", "r2", "t2", "r3", "fan", "sel"]
    bufs = {name: scratch[3 * n : 3 * n + 3] for n, name in enumerate(names)}
    flat, weight, w_sem, own_sem, s1, q1, s2, q2, s3, q3, s4, q4, s5, q5, s6, q6, out_sem = scratch[21:]
    me = lax.axis_index("edge")
    rep = lax.axis_index("rep")
    place = coords(me)
    barrier = pltpu.get_barrier_semaphore()
    for axis in range(3):
        for step in range(1, SIDE):
            peer, _ = moved(me, place, axis, step)
            pl.semaphore_signal(barrier, inc=1, device_id=(peer, rep), device_id_type=MESH)
    load = pltpu.make_async_copy(w_hbm.at[layer_block], weight, w_sem)
    load.start()

    def spot(g, va, vb, vc):
        index = [None] * 3
        for axis, value in zip(GROUP_AXES[g], (va, vb, vc)):
            index[axis] = value
        return tuple(index)

    def number(g, va, vb, vc):
        x, z, y = spot(g, va, vb, vc)
        return x * 16 + z * 4 + y

    def rows_of(g):
        return pl.ds(GROUP_ROWS[g][0], GROUP_ROWS[g][1])

    every = pl.ds(0, SIDE)
    send = pltpu.make_async_remote_copy
    here = [[place[axis] for axis in GROUP_AXES[g]] for g in range(3)]
    started = []

    own_copies = {}
    for j in range(SIDE):
        for g in range(3):
            ha, hb, hc = here[g]
            vb = (hb + 1 + j) % SIDE
            copy = pltpu.make_async_copy(
                sums.at[spot(g, ha, vb, every) + (rows_of(g),)], bufs["r1"][g].at[0, j], own_sem.at[g, j]
            )
            copy.start()
            own_copies[g, j] = copy
    pl.semaphore_wait(barrier, 9)

    in1 = {}
    for j in range(SIDE):
        for k in (2, 1, 3):
            for g in range(3):
                ha, hb, hc = here[g]
                peer, va = moved(me, place, GROUP_AXES[g][0], k)
                vb = (hb + 1 + j) % SIDE
                copy = send(
                    src_ref=sums.at[spot(g, va, vb, every) + (rows_of(g),)],
                    dst_ref=bufs["r1"][g].at[k, j],
                    send_sem=s1.at[g, k, j],
                    recv_sem=q1.at[g, k, j],
                    device_id=(peer, rep),
                    device_id_type=MESH,
                )
                copy.start()
                in1[g, k, j] = copy
                started.append(copy)

    in2 = {}
    for j in range(SIDE):
        for g in range(3):
            ha, hb, hc = here[g]
            n = GROUP_ROWS[g][1]
            axis_a = GROUP_AXES[g][0]
            vb = (hb + 1 + j) % SIDE
            own_copies[g, j].wait()
            for k in range(1, SIDE):
                in1[g, k, j].wait_recv()
            r1, t1 = bufs["r1"][g], bufs["t1"][g]

            def one(m, carry, g=g, j=j, ha=ha, hb=hb, hc=hc, vb=vb, axis_a=axis_a, r1=r1, t1=t1, n=n):
                dest = number(g, ha, vb, m)
                low = jnp.zeros((n, 128), F32)
                high = jnp.zeros((n, 128), F32)
                for k in range(SIDE):
                    source = (ha - k + SIDE) % SIDE
                    bit = bits[axis_a * SIDE + source, dest].astype(F32)
                    value = r1[k, j, m].astype(F32)
                    upper = value * bit
                    high = high + upper
                    low = low + (value - upper)
                t1[j, m, 0] = low.astype(BF16)
                t1[j, m, 1] = high.astype(BF16)
                return carry

            lax.fori_loop(0, SIDE, one, 0)
            if j < SIDE - 1:
                peer, _ = moved(me, place, GROUP_AXES[g][1], 1 + j)
                for i in range(SIDE):
                    vc = (hc + 1 + i) % SIDE
                    copy = send(
                        src_ref=t1.at[j, vc],
                        dst_ref=bufs["r2"][g].at[j, vc],
                        send_sem=s2.at[g, j, i],
                        recv_sem=q2.at[g, j, i],
                        device_id=(peer, rep),
                        device_id_type=MESH,
                    )
                    copy.start()
                    in2[g, j, i] = copy
                    started.append(copy)

    in3 = {}
    for i in range(SIDE):
        for g in range(3):
            ha, hb, hc = here[g]
            vc = (hc + 1 + i) % SIDE
            for j in range(SIDE - 1):
                in2[g, j, i].wait_recv()
            t1, r2, t2 = bufs["t1"][g], bufs["r2"][g], bufs["t2"][g]
            for slot in range(AB_DEV):
                value = t1[SIDE - 1, vc, slot].astype(F32)
                for j in range(SIDE - 1):
                    value = value + r2[j, vc, slot].astype(F32)
                t2[i, slot] = value.astype(BF16)
            if i < SIDE - 1:
                peer, _ = moved(me, place, GROUP_AXES[g][2], 1 + i)
                copy = send(
                    src_ref=t2.at[i],
                    dst_ref=bufs["r3"][g].at[i],
                    send_sem=s3.at[g, i],
                    recv_sem=q3.at[g, i],
                    device_id=(peer, rep),
                    device_id_type=MESH,
                )
                copy.start()
                in3[g, i] = copy
                started.append(copy)

    for g in range(3):
        for i in range(SIDE - 1):
            in3[g, i].wait_recv()
        t2, r3 = bufs["t2"][g], bufs["r3"][g]
        for slot in range(AB_DEV):
            value = t2[SIDE - 1, slot].astype(F32)
            for i in range(SIDE - 1):
                value = value + r3[i, slot].astype(F32)
            flat[slot, rows_of(g), :] = value.astype(BF16)

    load.wait()
    for slot in range(AB_DEV):
        gathered = jnp.concatenate([flat[slot, k * 128 : (k + 1) * 128, :] for k in range(4)], axis=1)
        update = silu(jnp.dot(gathered, weight[...], preferred_element_type=F32))
        rows = slice(slot * ABLK, (slot + 1) * ABLK)
        fresh = (atoms[rows, :].astype(F32) + update).astype(BF16)
        atoms_out[rows, :] = fresh
        for k in range(4):
            flat[slot, k * 128 : (k + 1) * 128, :] = fresh[:, k * 128 : (k + 1) * 128]
    in4 = {}

    def hop(g, axis_at, step, source, target, send_sem, recv_sem):
        peer, _ = moved(me, place, GROUP_AXES[g][axis_at], step)
        copy = send(
            src_ref=source,
            dst_ref=target,
            send_sem=send_sem,
            recv_sem=recv_sem,
            device_id=(peer, rep),
            device_id_type=MESH,
        )
        copy.start()
        started.append(copy)
        return copy

    def half(g, which):
        n = GROUP_ROWS[g][1]
        cut = (n // 32) * 16 + (n // 16) % 2 * 16
        return pl.ds(0, cut) if which == 0 else pl.ds(cut, n - cut)

    both = pl.ds(0, AB_DEV)
    for g in range(3):
        fan = bufs["fan"][g]
        fan[0, 0] = flat[:, rows_of(g), :]
        for k in (1, 3):
            in4[g, k] = hop(g, 2, k, fan.at[0, 0], fan.at[0, k], s4.at[g, k], q4.at[g, k])
    on4 = {}
    for g in range(3):
        fan = bufs["fan"][g]
        for which, k in enumerate((1, 3)):
            in4[g, k].wait_recv()
            rows = half(g, which)
            on4[g, which] = hop(
                g,
                2,
                k,
                fan.at[0, k, both, rows],
                fan.at[0, 2, both, rows],
                s4.at[g, 2 * which],
                q4.at[g, 2 * which],
            )

    in5 = {}
    for i in (0, 1, 3, 2):
        for g in range(3):
            fan = bufs["fan"][g]
            if i == 2:
                on4[g, 0].wait_recv()
                on4[g, 1].wait_recv()
            for k in (1, 3):
                in5[g, k, i] = hop(g, 1, k, fan.at[0, i], fan.at[k, i], s5.at[g, k, i], q5.at[g, k, i])
    on5 = {}

    def forward():
        for i in (0, 1, 3, 2):
            for g in range(3):
                fan = bufs["fan"][g]
                for which, k in enumerate((1, 3)):
                    in5[g, k, i].wait_recv()
                    rows = half(g, which)
                    on5[g, which, i] = hop(
                        g,
                        1,
                        k,
                        fan.at[k, i, both, rows],
                        fan.at[2, i, both, rows],
                        s5.at[g, 2 * which, i],
                        q5.at[g, 2 * which, i],
                    )

    out_copies = []
    in6 = []
    for j in (0, 1, 3, 2):
        if j == 1:
            forward()
        for g in range(3):
            ha, hb, hc = here[g]
            fan, sel = bufs["fan"][g], bufs["sel"][g]
            axis_a = GROUP_AXES[g][0]
            if j == 2:
                for i in range(SIDE):
                    on5[g, 0, i].wait_recv()
                    on5[g, 1, i].wait_recv()
            vb = (hb - j + SIDE) % SIDE

            def choose(m, carry, g=g, j=j, ha=ha, hc=hc, vb=vb, axis_a=axis_a, fan=fan, sel=sel):
                vc = (hc - m + SIDE) % SIDE
                dest = number(g, ha, vb, vc)
                for k in range(SIDE):
                    bit = bits[axis_a * SIDE + (ha + k) % SIDE, dest]
                    sel[k, j, vc] = jnp.where(bit > 0, fan[j, m, 1], fan[j, m, 0])
                return carry

            lax.fori_loop(0, SIDE, choose, 0)
            target = home.at[spot(g, ha, vb, every) + (rows_of(g),)]
            for k in (2, 1, 3):
                peer, _ = moved(me, place, axis_a, k)
                copy = send(
                    src_ref=sel.at[k, j],
                    dst_ref=target,
                    send_sem=s6.at[g, k, j],
                    recv_sem=q6.at[g, k, j],
                    device_id=(peer, rep),
                    device_id_type=MESH,
                )
                copy.start()
                in6.append(copy)
                started.append(copy)
            copy = pltpu.make_async_copy(sel.at[0, j], target, out_sem.at[g, j])
            copy.start()
            out_copies.append(copy)

    for copy in out_copies:
        copy.wait()
    for copy in in6:
        copy.wait_recv()
    for copy in started:
        copy.wait_send()


def atom_round(layer_block, sums, w_atom, atoms, bits):
    feat = atoms.shape[1]
    vmem = pl.BlockSpec(memory_space=pltpu.VMEM)
    anywhere = pl.BlockSpec(memory_space=pl.ANY)

    def per_group(*lead):
        return [pltpu.VMEM(lead + (n, 128), BF16) for _, n in GROUP_ROWS]

    dma = pltpu.SemaphoreType.DMA
    scratch = (
        per_group(4, 4, 4)
        + per_group(4, 4, 2)
        + per_group(3, 4, 2)
        + per_group(4, 2)
        + per_group(3, 2)
        + per_group(4, 4, 2)
        + per_group(4, 4, 4)
        + [
            pltpu.VMEM((2, 512, 128), BF16),
            pltpu.VMEM((feat, feat), BF16),
            dma,
            dma((3, 4)),
            dma((3, 4, 4)),
            dma((3, 4, 4)),
            dma((3, 3, 4)),
            dma((3, 3, 4)),
            dma((3, 3)),
            dma((3, 3)),
            dma((3, 4)),
            dma((3, 4)),
            dma((3, 4, 4)),
            dma((3, 4, 4)),
            dma((3, 4, 4)),
            dma((3, 4, 4)),
            dma((3, 4)),
        ]
    )
    home, fresh = pl.pallas_call(
        functools.partial(atoms_kernel, layer_block),
        out_shape=(
            jax.ShapeDtypeStruct((SIDE, SIDE, SIDE, 512, 128), BF16),
            jax.ShapeDtypeStruct(atoms.shape, BF16),
        ),
        in_specs=[pl.BlockSpec(memory_space=pltpu.SMEM), anywhere, anywhere, vmem],
        out_specs=(anywhere, vmem),
        scratch_shapes=scratch,
        name=f"atoms{layer_block}",
        compiler_params=pltpu.CompilerParams(
            collective_id=BLOCKS + layer_block, has_side_effects=True, vmem_limit_bytes=56 << 20
        ),
    )(bits, sums.reshape(SIDE, SIDE, SIDE, 512, 128), w_atom, atoms)
    return home.reshape(PEERS, 512, 128), fresh


def fetch_kernel(owner, first, last, msg, third, keys, home, out, column, blocks, acc, ready, sems):
    count = owner.shape[0]
    step = pl.program_id(0)

    def copy(l):
        return pltpu.make_async_copy(home.at[owner[l]], blocks.at[l], sems.at[l])

    @pl.when(step == 0)
    def _():
        def begin(l, carry):
            copy(l).start()
            return carry

        lax.fori_loop(0, count, begin, 0)
        ready[0] = 0
        to_column(keys, column)

    def finish(l, carry):
        copy(l).wait()
        return carry

    final = step * 4 + 3
    needed = jnp.where(step == 3, count, jnp.minimum(last[final] + 4, count))
    lax.fori_loop(ready[0], needed, finish, 0)
    ready[0] = needed

    for t in range(4):
        tile = step * 4 + t
        rows = pl.ds(t * 128, 128)
        low = first[tile]

        def part(base):
            want = base * ABLK + lax.broadcasted_iota(jnp.int32, (128, 512), 1)
            key = column[pl.ds(pl.multiple_of(tile * 128, 128), 128), :]
            pick = (key == want).astype(F32).astype(BF16)
            at = [jnp.minimum(base + j, count - 1) for j in range(4)]
            block = jnp.concatenate(
                [
                    jnp.concatenate([blocks[at[j], k * 128 : (k + 1) * 128, :] for k in range(4)], axis=1)
                    for j in range(4)
                ],
                axis=0,
            )
            return jnp.dot(pick, block, preferred_element_type=F32)

        base = msg[rows, :].astype(F32) + third[rows, :].astype(F32)
        found = part(low)
        out[rows, :] = (base + found).astype(BF16)

        @pl.when(last[tile] >= low + 4)
        def _():
            acc[...] = msg[rows, :].astype(F32) + third[rows, :].astype(F32) + part(low)

            def more(i, carry):
                acc[...] += part(low + 4 * i)
                return carry

            lax.fori_loop(1, (last[tile] - low) // 4 + 1, more, 0)
            out[rows, :] = acc[...].astype(BF16)


def fetch(message, third, keys, home, owner, first, last):
    rows, feat = message.shape
    lists = owner.shape[0]
    block = pl.BlockSpec((512, feat), lambda i, *_: (i, 0))
    return pl.pallas_call(
        fetch_kernel,
        out_shape=jax.ShapeDtypeStruct((rows, feat), BF16),
        grid_spec=pltpu.PrefetchScalarGridSpec(
            num_scalar_prefetch=3,
            grid=(rows // 512,),
            in_specs=[
                block,
                block,
                pl.BlockSpec((16, 128), lambda i, *_: (0, 0)),
                pl.BlockSpec(memory_space=pl.ANY),
            ],
            out_specs=block,
            scratch_shapes=[
                pltpu.VMEM((rows, 1), jnp.int32),
                pltpu.VMEM((lists, 512, 128), BF16),
                pltpu.VMEM((128, feat), F32),
                pltpu.SMEM((1,), jnp.int32),
                pltpu.SemaphoreType.DMA((lists,)),
            ],
        ),
        name="fetch",
        compiler_params=pltpu.CompilerParams(dimension_semantics=("arbitrary",)),
    )(owner, first, last, message, third, keys, home)


def on_device(
    edge_feats,
    atom_feats,
    w_edge,
    w_atom,
    send_order,
    recv_pos,
    edge_list,
    edge_atom,
    list_block,
    block_home,
):
    lists = list_block.shape[1]
    list_table = jnp.arange(lists, dtype=jnp.int32)
    peer_table = jnp.arange(PEERS, dtype=jnp.int32)
    block_table = jnp.arange(block_home.shape[0], dtype=jnp.int32)
    list_place = jnp.sum(
        jnp.where(list_block[0][:, None] == block_table[None, :], block_home[None, :], 0), axis=1
    )
    owner = list_place // AB_DEV
    placing = owner[None, :] == peer_table[:, None]
    list_of = jnp.max(jnp.where(placing, list_table[None, :], -1), axis=1)
    slot_of = jnp.sum(jnp.where(placing, (list_place % AB_DEV)[None, :], 0), axis=1)
    edge_lists = edge_list[0]
    start = jnp.sum((edge_lists[None, :] < list_table[:, None]).astype(jnp.int32), axis=1)
    tiled_lists = edge_lists.reshape(16, 128)
    first, last = tiled_lists[:, 0], tiled_lists[:, 127]
    keys = edge_lists * ABLK + edge_atom[0]
    keys = keys.reshape(16, 128)
    order = send_order.reshape(-1)
    places = recv_pos.reshape(-1)
    ids = jnp.broadcast_to(jnp.pad(slot_of, (0, 128 - PEERS))[None, :], (8, 128))
    message, atoms = edge_feats, atom_feats
    for layer_block in range(BLOCKS):
        pair, all_ids = exchange(layer_block, message, w_edge, order, places, ids)
        if layer_block == 0:
            bits = all_ids[:, 0, :]
        third, sums = list_sums(layer_block, pair, w_edge, keys, list_of, owner, start)
        home, atoms = atom_round(layer_block, sums, w_atom, atoms, bits)
        message = fetch(message, third, keys, home, owner, first, last)
    return message, atoms


def solution(mesh):
    split = P(("rep", "edge"), None)
    whole = P(None, None, None)
    return jax.shard_map(
        on_device,
        mesh=mesh,
        in_specs=(split, split, whole, whole, split, split, split, split, split, P("rep")),
        out_specs=(split, split),
        check_vma=False,
    )
```
